32 devices in a mesh: tiles: 2 (over y), space: 4 (over x, core), particle: 4 (over z).
Axes of the slice: x: 2, y: 2, z: 4, core: 2. Of those that a mesh axis runs over, the one named last changes fastest.
Arguments:
- states: float32 [8, 6, 32, 512], P(('tiles', 'particle'), None, 'space'), parts along dimension 0, may hold values from -6 to 6
- noise: float32 [8, 6, 32, 512], P(('tiles', 'particle'), None, 'space'), parts along dimension 0, may hold values from -6 to 6
- observed: float32 [12, 32, 512], P('tiles', 'space'), parts along dimension 0, may hold values from -6 to 6
- inv_var: float32 [12, 32, 512], P('tiles', 'space'), parts along dimension 0, may hold values from 0.5 to 2
- psf_bank: float32 [16, 6, 5, 5], P('tiles'), parts along dimension 0, may hold values from 0 to 0.1
- psf_ids: int32 [64, 4], P(('tiles', 'space')), parts along dimension 0, may hold values from 0 to 7
- ancestors: int32 [8, 4], P(('tiles', 'particle'), 'space'), parts along dimension 0, may hold values from 0 to 3
- carried: float32 [8], P(('tiles', 'particle')), parts along dimension 0, may hold values from 276 to 546
- stem_w1: bfloat16 [128, 6, 3, 3], replicated, may hold values from -0.875 to 0.875
- stem_b1: float32 [128], replicated, may hold values from -3 to 3
- stem_w2: bfloat16 [128, 128, 3, 3], replicated, may hold values from -0.1875 to 0.1875
- stem_b2: float32 [128], replicated, may hold values from -3 to 3
- head_w: bfloat16 [6, 128], replicated, may hold values from -0.5 to 0.5
Outputs:
- next_states: float32 [8, 6, 32, 512], P(('tiles', 'particle'), None, 'space'), parts along dimension 0
- log_weight: float32 [8], P(('tiles', 'particle')), parts along dimension 0
The draws below stay inside these ranges and needn't reach their ends.
There are 2 independent parts, one for each index of `tiles`. The reference program is written for one: setup_inputs(seed, part) draws one part's arguments, and reference() takes and returns one part's arrays. A program takes and returns all parts, laid end to end along the dimension named above; an argument that names none is the same for every part. Nothing has to cross between parts.
Inputs may be any that keep to these rules, and one draw needn't show every extreme that they name: psf_ids[i, j] names the stencil of columns 128 * j to 128 * (j + 1) - 1 of row i. ancestors[p, s] is the particle whose strip s becomes strip s of particle p.
All inputs are finite; a program needn't handle non-finite values.
Results may differ from the reference program's by a relative error of at most 0.0013.
Values may be sent and summed in bfloat16 or wider, within the bound.
A program may use at most 64 MiB of HBM per device.

```python
import math
import jax
import jax.numpy as jnp
import numpy as np
from jax import lax

BANDS = 6
CHANNELS = 128
NPSF = 8
KERNEL = 5
BLOCK = 128
ROWS_DEV = 8
COLS = 512
PARTICLES = 4
STRIPS = 4
IMAGE_ROWS = 32


def draw_carried(key, part):
    first_key = jax.random.fold_in(key, 11)
    second_key = jax.random.fold_in(key, 12)
    order_key = jax.random.fold_in(key, 13)
    pixel_count = BANDS * IMAGE_ROWS * COLS
    parity = (jnp.asarray(part, jnp.int32) % 2).astype(jnp.float32)
    base = jnp.float32(200.0 + pixel_count // 1024) + 250.0 * parity
    offsets = -jax.random.uniform(first_key, (PARTICLES,), jnp.float32, 4.0, 20.0)
    runner = -jax.random.uniform(second_key, (), jnp.float32, 1.0, 3.0)
    offsets = offsets.at[0].set(0.0).at[1].set(runner).at[2].set(-20.0)
    order = jax.random.permutation(order_key, jnp.arange(PARTICLES, dtype=jnp.int32))
    return base + offsets[order]


def with_ends(values, own_key, low, top_value):
    longest = values.shape.index(max(values.shape))
    spots = []
    for shift in (0, 1):
        where = [jax.random.randint(jax.random.fold_in(own_key, axis), (), 0, length) for axis, length in enumerate(values.shape)]
        where[longest] = (where[longest] + shift) % values.shape[longest]
        spots.append(tuple(where))
    return values.at[spots[0]].set(low).at[spots[1]].set(top_value)


def levels(stream_key, extent, pieces, least, top_value):
    def one(position, blocks):
        draws = jax.random.uniform(jax.random.fold_in(jax.random.fold_in(stream_key, 6), position), (blocks,), jnp.float32, least / len(pieces), top_value / len(pieces))
        return jnp.repeat(jnp.exp(draws), extent[position] // blocks).reshape((-1,) + (1,) * (len(extent) - position - 1))

    factor_of = one(*pieces[0])
    for cut in pieces[1:]:
        factor_of = factor_of * one(*cut)
    return factor_of


def rank_table(number_of, slope):
    portions = [(1 << 20) // math.isqrt(standing ** slope) + 1 for standing in range(1, number_of + 1)]
    scale = 1 + sum(portions) // (1 << 30)
    return np.cumsum(np.array([max(1, weight // scale) for weight in portions]))


def skewed_ids(rng, shape, count, skew):
    grid = rank_table(count, skew)
    lot = jax.random.randint(jax.random.fold_in(rng, 1), shape, 0, int(grid[count - 1]))
    grade = jnp.searchsorted(jnp.asarray(grid, jnp.int32), lot, side="right")
    return jax.random.permutation(jax.random.fold_in(rng, 2), count)[grade].astype(jnp.int32)


def normal_values(rng, dims, scale, limit, shards=(), held_as=jnp.bfloat16):
    result = scale * jax.random.normal(rng, dims, jnp.float32)
    if shards:
        result = result * levels(rng, dims, shards, -0.22, 0.18)
    return jnp.clip(result, -limit, limit).astype(held_as)


def setup_inputs(seed: int = 0, part: int = 0) -> dict:
    keys = jax.random.split(jax.random.key(seed), 14)
    part_splits = jax.random.split(jax.random.fold_in(keys[13], part), 14)
    states = normal_values(part_splits[0], (PARTICLES, BANDS, IMAGE_ROWS, COLS), 1.0, 6.0, ((0, 4), (2, 4)), jnp.float32)
    noise = normal_values(part_splits[1], (PARTICLES, BANDS, IMAGE_ROWS, COLS), 1.0, 6.0, ((0, 4), (2, 4)), jnp.float32)
    observed = normal_values(part_splits[2], (BANDS, IMAGE_ROWS, COLS), 1.0, 6.0, ((1, 4),), jnp.float32)
    inv_var = jnp.clip(jnp.exp(math.log(2.0) - 1.3862944 * jax.random.uniform(part_splits[3], (BANDS, IMAGE_ROWS, COLS), jnp.float32) ** levels(part_splits[3], (BANDS, IMAGE_ROWS, COLS), ((1, 4),), -0.2, 0.2)), 0.5, 2.0)
    psf_bank = jnp.clip(jax.random.uniform(part_splits[4], (NPSF, BANDS, KERNEL, KERNEL), jnp.float32, 0.0, 0.1), 0.0, 0.1)
    psf_ids = with_ends(jax.random.randint(part_splits[5], (IMAGE_ROWS, COLS // BLOCK), 0, NPSF), jax.random.fold_in(part_splits[5], 1), 0, NPSF - 1).astype(jnp.int32)
    ancestors = with_ends(skewed_ids(part_splits[6], (PARTICLES, STRIPS), PARTICLES, 1), jax.random.fold_in(part_splits[6], 3), 0, PARTICLES - 1).astype(jnp.int32)
    carried = draw_carried(jax.random.fold_in(jax.random.fold_in(keys[13], part), 71), part)
    stem_w1 = normal_values(keys[8], (CHANNELS, BANDS, 3, 3), (9 * BANDS) ** -0.5, 0.875)
    stem_b1 = normal_values(keys[9], (CHANNELS,), 0.5, 3.0, (), jnp.float32)
    stem_w2 = normal_values(keys[10], (CHANNELS, CHANNELS, 3, 3), (9 * CHANNELS) ** -0.5, 0.1875)
    stem_b2 = normal_values(keys[11], (CHANNELS,), 0.5, 3.0, (), jnp.float32)
    head_w = normal_values(keys[12], (BANDS, CHANNELS), CHANNELS ** -0.5, 0.5)
    return {"states": states, "noise": noise, "observed": observed, "inv_var": inv_var, "psf_bank": psf_bank, "psf_ids": psf_ids, "ancestors": ancestors, "carried": carried, "stem_w1": stem_w1, "stem_b1": stem_b1, "stem_w2": stem_w2, "stem_b2": stem_b2, "head_w": head_w}


ALPHA_ROOT = 0.8
NOISE_ROOT = 0.6
GUIDE = 0.5
SPREAD = 0.3

def correlate(field, kernel, groups):
    return lax.conv_general_dilated(field, kernel, (1, 1), 'SAME', dimension_numbers=('NCHW', 'OIHW', 'NCHW'), feature_group_count=groups, precision=lax.Precision.HIGHEST)

def blur_map(estimate, masks, psf_bank):
    summed = jnp.zeros_like(estimate)
    for kind in range(NPSF):
        stencil = psf_bank[kind][:, None]
        summed = summed + masks[kind][None] * correlate(estimate[None], stencil, BANDS)[0]
    return summed

def reference(states, noise, observed, inv_var, psf_bank, psf_ids, ancestors, carried, stem_w1, stem_b1, stem_w2, stem_b2, head_w):
    tiled = states.reshape(PARTICLES, BANDS, STRIPS, ROWS_DEV, COLS)
    picked = tiled[ancestors, :, jnp.arange(STRIPS)[None, :]]
    resampled = picked.transpose(0, 2, 1, 3, 4).reshape(PARTICLES, BANDS, IMAGE_ROWS, COLS)
    id_cells = jnp.repeat(psf_ids, BLOCK, axis=1)
    masks = (id_cells[None] == jnp.arange(NPSF, dtype=jnp.int32)[:, None, None]).astype(jnp.float32)
    first_kernel = stem_w1.astype(jnp.float32)
    second_kernel = stem_w2.astype(jnp.float32)
    head_matrix = head_w.astype(jnp.float32)
    temper = 1.0 / math.sqrt(BANDS * IMAGE_ROWS * COLS)

    def one_particle(triple):
        current, fresh, prior = triple
        rounded = lax.optimization_barrier(current.astype(jnp.bfloat16)).astype(jnp.float32)
        layer_one = jax.nn.silu(correlate(rounded[None], first_kernel, 1)[0] + stem_b1[:, None, None])
        layer_one = lax.optimization_barrier(layer_one.astype(jnp.bfloat16)).astype(jnp.float32)
        layer_two = jax.nn.silu(correlate(layer_one[None], second_kernel, 1)[0] + stem_b2[:, None, None])
        layer_two = lax.optimization_barrier(layer_two.astype(jnp.bfloat16)).astype(jnp.float32)
        correction = jnp.einsum('bc,chw->bhw', head_matrix, layer_two, precision=lax.Precision.HIGHEST)
        estimate = (current - NOISE_ROOT * correction) / ALPHA_ROOT
        blurred = blur_map(estimate, masks, psf_bank)
        misfit = observed - blurred
        residual = inv_var * misfit
        _, pullback = jax.vjp(lambda field: blur_map(field, masks, psf_bank), estimate)
        gradient = pullback(residual)[0]
        likelihood = -0.5 * jnp.sum(residual * misfit)
        twist = jnp.sum(gradient * gradient)
        raw_weight = prior + temper * (likelihood + 0.5 * GUIDE * twist)
        moved = estimate + GUIDE * gradient + SPREAD * fresh
        return (moved, raw_weight)
    next_states, raw_weight = lax.map(one_particle, (resampled, noise, carried))
    highest = jnp.max(raw_weight)
    log_weight = raw_weight - highest - jnp.log(jnp.sum(jnp.exp(raw_weight - highest)))
    return (next_states, log_weight)
```

```python
import functools
import math

import jax
import jax.numpy as jnp
from jax import lax
from jax.experimental import pallas as pl
from jax.experimental.pallas import tpu as pltpu
from jax.sharding import PartitionSpec as P

ALPHA_ROOT = 0.8
NOISE_ROOT = 0.6
GUIDE = 0.5
SPREAD = 0.3

MESH = pl.DeviceIdType.MESH
LANES = 128


def silu(x):
    half = 0.5 * x
    return half + half * jnp.tanh(half)


def shifted(x, step):
    if step == 0:
        return x
    axis = x.ndim - 1
    cols = x.shape[axis]
    lane = lax.broadcasted_iota(jnp.int32, x.shape, axis)
    moved = pltpu.roll(x, (-step) % cols, axis)
    keep = lane < cols - step if step > 0 else lane >= -step
    return jnp.where(keep, moved, 0.0)


def each(low, high, body):
    if high - low <= 16:
        for index in range(low, high):
            body(index)
    else:
        lax.fori_loop(low, high, lambda index, carry: (body(index), carry)[1], 0)


def step_kernel(
    strips, parts,
    anc_hbm, carried_hbm, states_hbm, noise_hbm, obs_hbm, iv_hbm, psf_hbm, ids_hbm,
    w1_hbm, b1_hbm, w2_hbm, b2_hbm, head_hbm,
    out_ref, logw_ref,
    anc_ref, carried_ref, states_ref, noise_ref, obs_ref, iv_ref, psf_ref,
    w1_ref, b1_ref, w2_ref, b2_ref, head_ref, w1t, w1k, in_sem,
    hi_g, lo_g, hi_h, lo_h, obs_h, iv_h, ids_h, ids_s, packs,
    xc, lo_rows, feats, w2s, corr, shifts, table, resid, obs_t, iv_t, bias,
    hi_send, hi_recv, lo_send, lo_recv, halo_send, halo_recv, pack_send, pack_recv, own_sem,
):
    bands, rows, cols = obs_ref.shape
    blocks = cols // LANES
    total = bands * rows
    channels = head_ref.shape[1]
    s = lax.axis_index("space")
    p = lax.axis_index("particle")
    me = s * parts + p
    count = strips * parts
    has_low = s > 0
    has_high = s < strips - 1

    fetches = [
        pltpu.make_async_copy(src, dst, in_sem.at[at])
        for at, (src, dst) in enumerate((
            (states_hbm, states_ref), (w1_hbm, w1_ref), (psf_hbm, psf_ref), (b1_hbm, b1_ref),
            (b2_hbm, b2_ref), (w2_hbm, w2_ref), (head_hbm, head_ref), (anc_hbm, anc_ref),
            (carried_hbm, carried_ref), (obs_hbm, obs_ref), (iv_hbm, iv_ref),
            (ids_hbm, ids_h.at[2]), (noise_hbm, noise_ref),
        ))
    ]
    for fetch in fetches:
        fetch.start()

    barrier = pltpu.get_barrier_semaphore()

    def greet(k):
        t = lax.rem(me + k, count)
        pl.semaphore_signal(
            barrier, inc=1,
            device_id={"space": t // parts, "particle": lax.rem(t, parts)},
            device_id_type=MESH,
        )

    each(1, count, greet)

    fetches[0].wait()
    state = states_ref[0].reshape(total, cols)
    high_part = state.astype(jnp.bfloat16)
    hi_g[p] = high_part
    lo_g[p] = (state - high_part.astype(jnp.float32)).astype(jnp.bfloat16)
    pl.semaphore_wait(barrier, count - 1)

    def gather_copy(buf, send, recv, k):
        return pltpu.make_async_remote_copy(
            src_ref=buf.at[p], dst_ref=buf.at[p],
            send_sem=send.at[k], recv_sem=recv.at[p],
            device_id={"particle": lax.rem(p + k, parts)}, device_id_type=MESH,
        )

    def gather_arrival(buf, send, recv, k):
        q = lax.rem(p + parts - k, parts)
        return pltpu.make_async_remote_copy(
            src_ref=buf.at[q], dst_ref=buf.at[q],
            send_sem=send.at[k], recv_sem=recv.at[q],
            device_id={"particle": q}, device_id_type=MESH,
        )

    for k in range(1, parts):
        gather_copy(hi_g, hi_send, hi_recv, k).start()

    def halo(kind, src, dst, side):
        towards = s + 1 if side == 0 else s - 1
        return pltpu.make_async_remote_copy(
            src_ref=src, dst_ref=dst.at[side],
            send_sem=halo_send.at[kind, side], recv_sem=halo_recv.at[kind, side],
            device_id={"space": towards}, device_id_type=MESH,
        )

    def start_halo(kind, src, dst):
        @pl.when(has_high)
        def _():
            halo(kind, src, dst, 0).start()

        @pl.when(has_low)
        def _():
            halo(kind, src, dst, 1).start()

    def await_halo(kind, src, dst):
        @pl.when(has_low)
        def _():
            halo(kind, src, dst, 0).wait_recv()

        @pl.when(has_high)
        def _():
            halo(kind, src, dst, 1).wait_recv()

    def end_halo(kind, src, dst):
        @pl.when(has_high)
        def _():
            halo(kind, src, dst, 0).wait_send()

        @pl.when(has_low)
        def _():
            halo(kind, src, dst, 1).wait_send()

    def blank(buf, side):
        buf[side] = jnp.zeros(buf.shape[1:], buf.dtype)

    for buf in (hi_h, lo_h, obs_h, iv_h, ids_h):
        @pl.when(jnp.logical_not(has_low))
        def _():
            blank(buf, 0)

        @pl.when(jnp.logical_not(has_high))
        def _():
            blank(buf, 1)

    for fetch in fetches[1:]:
        fetch.wait()
    w1t[...] = jnp.zeros(w1t.shape, jnp.float32)
    for band in range(bands):
        for dy in range(3):
            for dx in range(3):
                at = dy * 24 + dx * 8 + band
                w1t[at:at + 1, :] = w1_ref[band, dy, dx:dx + 1, :].astype(jnp.float32)
    w1k[...] = w1t[...].T[:, :72].astype(jnp.bfloat16)
    for dy in range(3):
        for dx in range(3):
            w2s[dx * channels:(dx + 1) * channels, dy * channels:(dy + 1) * channels] = w2_ref[dy, dx]
    bias[0] = jnp.broadcast_to(b1_ref[...], (channels, channels)).T
    bias[1] = jnp.broadcast_to(b2_ref[...], (channels, channels)).T
    bank = psf_ref[...]
    taps, kinds = bank.shape[0] * bank.shape[1], bank.shape[2]
    flat = bank.reshape(taps * kinds, bands)
    eye = (
        lax.broadcasted_iota(jnp.int32, (8, bands), 0)
        == lax.broadcasted_iota(jnp.int32, (8, bands), 1)
    ).astype(jnp.float32)
    columns = lax.dot_general(
        eye, flat, (((1,), (1,)), ((), ())),
        precision=lax.Precision.HIGHEST, preferred_element_type=jnp.float32,
    )
    for tap in range(taps):
        for kind in range(kinds):
            at = tap * kinds + kind
            table[kind, tap] = jnp.broadcast_to(columns[:, at:at + 1], (8, LANES))
    corr[...] = jnp.zeros(corr.shape, jnp.float32)
    obs_t[...] = jnp.zeros(obs_t.shape, jnp.float32)
    iv_t[...] = jnp.zeros(iv_t.shape, jnp.float32)
    lo_rows[...] = jnp.zeros(lo_rows.shape, jnp.float32)
    xc[...] = jnp.zeros(xc.shape, jnp.float32)

    def turned(x):
        return jnp.transpose(x, (1, 0, 2))

    def rows_of(flat_part):
        return turned(flat_part.astype(jnp.float32).reshape(bands, rows, cols))

    def fill_inputs(slot, part):
        value = rows_of(part)
        base = slot * rows
        for dx in range(3):
            xc[base:base + rows, dx * 8:dx * 8 + bands, :] = shifted(value, dx - 1)

    width = bias.shape[2]

    def spread(b):
        return jnp.concatenate([b] * (cols // width), axis=1)

    def first_layer(i, masked):
        window = xc[pl.ds(i - 1, 3)].reshape(72, cols).astype(jnp.bfloat16)
        mixed = jnp.dot(w1k[...], window, preferred_element_type=jnp.float32)
        value = silu(mixed + spread(bias[0]))
        if masked is not None:
            value = jnp.where(masked, value, 0.0)
        at = (i - 3) * channels
        feats[pl.ds(at if isinstance(at, int) else pl.multiple_of(at, channels), channels), :] = value.astype(jnp.bfloat16)

    for k in range(1, parts):
        gather_arrival(hi_g, hi_send, hi_recv, k).wait_recv()
    ancestor = anc_ref[0, 0]
    picked_hi = hi_g[ancestor]
    hi_h[2] = picked_hi
    start_halo(0, hi_h.at[2], hi_h)
    for k in range(1, parts):
        gather_copy(lo_g, lo_send, lo_recv, k).start()
    fill_inputs(1, picked_hi)

    @pl.loop(9, 15, unroll=3)
    def _(i):
        first_layer(i, None)

    def second_layer(e):
        window = feats[pl.ds(pl.multiple_of(e * channels, channels), 3 * channels), :]
        mixed = jnp.dot(w2s[...], window, preferred_element_type=jnp.float32)
        summed = (
            mixed[channels:2 * channels]
            + shifted(mixed[:channels], -1)
            + shifted(mixed[2 * channels:], 1)
        )
        hidden = silu(summed + spread(bias[1])).astype(jnp.bfloat16)
        corr[e, 0:bands, :] = jnp.dot(head_ref[...], hidden, preferred_element_type=jnp.float32)

    pl.loop(6, 10, unroll=4)(second_layer)
    await_halo(0, hi_h.at[2], hi_h)
    start_halo(4, ids_h.at[2], ids_h)
    start_halo(2, obs_ref, obs_h)
    start_halo(3, iv_ref, iv_h)
    fill_inputs(0, hi_h[0])
    fill_inputs(2, hi_h[1])

    @pl.loop(3, 8, unroll=5)
    def _(i):
        first_layer(i, has_low)

    first_layer(8, None)
    first_layer(15, None)

    @pl.loop(16, 21, unroll=5)
    def _(i):
        first_layer(i, has_high)

    pl.loop(0, 6, unroll=6)(second_layer)
    for k in range(1, parts):
        gather_arrival(lo_g, lo_send, lo_recv, k).wait_recv()
    lo_h[2] = lo_g[ancestor]
    start_halo(1, lo_h.at[2], lo_h)
    pl.loop(10, 16, unroll=6)(second_layer)

    lo_rows[rows:2 * rows, 0:bands, :] = rows_of(lo_h[2])
    await_halo(1, lo_h.at[2], lo_h)
    lo_rows[0:rows, 0:bands, :] = rows_of(lo_h[0])
    lo_rows[2 * rows:3 * rows, 0:bands, :] = rows_of(lo_h[1])
    await_halo(2, obs_ref, obs_h)
    await_halo(3, iv_ref, iv_h)
    await_halo(4, ids_h.at[2], ids_h)
    ids_copy = pltpu.make_async_copy(ids_h, ids_s, own_sem)
    ids_copy.start()
    for held, halo_buf, own in ((obs_t, obs_h, obs_ref), (iv_t, iv_h, iv_ref)):
        held[0:2, 0:bands, :] = turned(halo_buf[0])[rows - 2:rows]
        held[2:2 + rows, 0:bands, :] = turned(own[...])
        held[2 + rows:4 + rows, 0:bands, :] = turned(halo_buf[1])[0:2]

    @pl.loop(0, 16, unroll=4)
    def _(e):
        current = xc[e + 4, 8:16, :] + lo_rows[e + 4]
        value = (current - NOISE_ROOT * corr[e]) / ALPHA_ROOT
        there = jnp.logical_and(
            jnp.logical_or(e >= 4, has_low), jnp.logical_or(e < 4 + rows, has_high)
        )
        value = jnp.where(there, value, 0.0)
        for dx in range(5):
            shifts[e, dx] = shifted(value, dx - 2)

    ids_copy.wait()

    def kind_of(q, j):
        low, high = q < 2, q >= 2 + rows
        slot = jnp.where(low, 0, jnp.where(high, 1, 2))
        row = jnp.where(low, rows - 2 + q, jnp.where(high, q - 2 - rows, q - 2))
        return ids_s[slot, j, row]

    @pl.loop(0, rows + 4, unroll=2)
    def _(q):
        there = jnp.logical_and(
            jnp.logical_or(q >= 2, has_low), jnp.logical_or(q < 2 + rows, has_high)
        )
        for j in range(blocks):
            kind = kind_of(q, j)
            lanes = slice(j * LANES, (j + 1) * LANES)
            sums = []
            for dy in range(5):
                term = None
                for dx in range(5):
                    product = table[kind, dy * 5 + dx] * shifts[q + dy, dx, :, lanes]
                    term = product if term is None else term + product
                sums.append(term)
            blurred = sums[0] + sums[1] + sums[2] + sums[3] + sums[4]
            misfit = obs_t[q, :, lanes] - blurred
            residual = iv_t[q, :, lanes] * misfit
            resid[q, :, lanes] = jnp.where(there, residual, 0.0)
            obs_t[q, :, lanes] = residual * misfit

    def adjoint(y, twist):
        moved = []
        for dx in range(5):
            pieces = []
            for j in range(blocks):
                lanes = slice(j * LANES, (j + 1) * LANES)
                term = None
                for dy in range(5):
                    q = y + 4 - dy
                    product = table[kind_of(q, j), dy * 5 + dx] * resid[q, :, lanes]
                    term = product if term is None else term + product
                pieces.append(term)
            moved.append(shifted(jnp.concatenate(pieces, axis=1), 2 - dx))
        gradient = moved[0] + moved[1] + moved[2] + moved[3] + moved[4]
        corr[y] = shifts[y + 4, 2] + GUIDE * gradient
        return twist + gradient * gradient

    twist = lax.fori_loop(0, rows, adjoint, jnp.zeros((8, cols), jnp.float32), unroll=2)
    energy = jnp.sum(obs_t[2:2 + rows], axis=0)
    mixed = -0.5 * energy + (0.5 * GUIDE) * twist
    partial = jnp.sum(mixed, axis=(0, 1), keepdims=True)
    temper = 1.0 / math.sqrt(bands * rows * strips * cols)
    prior = jnp.where(has_low, 0.0, carried_ref[0])
    packs[me] = jnp.broadcast_to(partial * temper, (8, LANES)) + prior

    def pack_copy(k):
        t = lax.rem(me + k, count)
        return pltpu.make_async_remote_copy(
            src_ref=packs.at[me], dst_ref=packs.at[me],
            send_sem=pack_send.at[k], recv_sem=pack_recv.at[me],
            device_id={"space": t // parts, "particle": lax.rem(t, parts)},
            device_id_type=MESH,
        )

    def pack_arrival(k):
        t = lax.rem(me + count - k, count)
        return pltpu.make_async_remote_copy(
            src_ref=packs.at[t], dst_ref=packs.at[t],
            send_sem=pack_send.at[k], recv_sem=pack_recv.at[t],
            device_id={"space": t // parts, "particle": lax.rem(t, parts)},
            device_id_type=MESH,
        )

    each(1, count, lambda k: pack_copy(k).start())

    moved = turned(corr[0:rows])
    out_ref[0] = moved[0:bands] + SPREAD * noise_ref[0]

    for k in range(1, parts):
        gather_copy(hi_g, hi_send, hi_recv, k).wait_send()
        gather_copy(lo_g, lo_send, lo_recv, k).wait_send()
    end_halo(0, hi_h.at[2], hi_h)
    end_halo(1, lo_h.at[2], lo_h)
    end_halo(2, obs_ref, obs_h)
    end_halo(3, iv_ref, iv_h)
    end_halo(4, ids_h.at[2], ids_h)

    each(1, count, lambda k: pack_arrival(k).wait_recv())
    raw = packs[0:parts]
    mine = packs[p]
    for strip in range(1, strips):
        raw = raw + packs[strip * parts:(strip + 1) * parts]
        mine = mine + packs[strip * parts + p]
    highest = jnp.max(raw, axis=0)
    summed = jnp.sum(jnp.exp(raw - highest[None]), axis=0)
    logw_ref[...] = (mine - highest - jnp.log(summed))[0:1, 0:1]
    each(1, count, lambda k: pack_copy(k).wait_send())


def deliver_kernel(moved_ref, logw_ref, out_hbm, logw_hbm, logw_line, sem):
    states_copy = pltpu.make_async_copy(moved_ref, out_hbm, sem.at[0])
    states_copy.start()
    logw_line[...] = logw_ref[0, 0:1]
    logw_copy = pltpu.make_async_copy(logw_line, logw_hbm, sem.at[1])
    logw_copy.start()
    states_copy.wait()
    logw_copy.wait()


def local(
    strips, parts,
    states, noise, observed, inv_var, psf_bank, psf_ids, ancestors, carried,
    stem_w1, stem_b1, stem_w2, stem_b2, head_w,
):
    bands, rows, cols = observed.shape
    channels = stem_w1.shape[0]
    kinds = psf_bank.shape[0]
    count = strips * parts
    flat = (bands * rows, cols)
    vmem = pl.BlockSpec(memory_space=pltpu.VMEM)
    hbm = pl.BlockSpec(memory_space=pltpu.HBM)
    bf, f32 = jnp.bfloat16, jnp.float32
    dma = pltpu.SemaphoreType.DMA
    next_states, log_weight = pl.pallas_call(
        functools.partial(step_kernel, strips, parts),
        out_shape=(
            pltpu.VMEM(states.shape, f32),
            pltpu.VMEM((1, 1), f32),
        ),
        in_specs=[hbm] * 13,
        out_specs=(vmem, vmem),
        scratch_shapes=[
            pltpu.SMEM((1, 1), jnp.int32),
            pltpu.SMEM((1,), f32),
            pltpu.VMEM(states.shape, f32),
            pltpu.VMEM(states.shape, f32),
            pltpu.VMEM(observed.shape, f32),
            pltpu.VMEM(observed.shape, f32),
            pltpu.VMEM((5, 5, kinds, bands), f32),
            pltpu.VMEM((bands, 3, 3, channels), bf),
            pltpu.VMEM((1, channels), f32),
            pltpu.VMEM((3, 3, channels, channels), bf),
            pltpu.VMEM((1, channels), f32),
            pltpu.VMEM((bands, channels), bf),
            pltpu.VMEM((LANES, channels), f32),
            pltpu.VMEM((channels, 72), bf),
            dma((13,)),
            pltpu.VMEM((parts,) + flat, bf),
            pltpu.VMEM((parts,) + flat, bf),
            pltpu.VMEM((3,) + flat, bf),
            pltpu.VMEM((3,) + flat, bf),
            pltpu.VMEM((2, bands, rows, cols), f32),
            pltpu.VMEM((2, bands, rows, cols), f32),
            pltpu.VMEM((3, psf_ids.shape[1], rows), jnp.int32),
            pltpu.SMEM((3, psf_ids.shape[1], rows), jnp.int32),
            pltpu.VMEM((count, 8, LANES), f32),
            pltpu.VMEM((3 * rows, 24, cols), f32),
            pltpu.VMEM((3 * rows, 8, cols), f32),
            pltpu.VMEM((18 * channels, cols), bf),
            pltpu.VMEM((3 * channels, 3 * channels), bf),
            pltpu.VMEM((16, 8, cols), f32),
            pltpu.VMEM((16, 5, 8, cols), f32),
            pltpu.VMEM((kinds, 25, 8, LANES), f32),
            pltpu.VMEM((rows + 4, 8, cols), f32),
            pltpu.VMEM((rows + 4, 8, cols), f32),
            pltpu.VMEM((rows + 4, 8, cols), f32),
            pltpu.VMEM((2, channels, channels), f32),
            dma((parts,)), dma((parts,)), dma((parts,)), dma((parts,)),
            dma((5, 2)), dma((5, 2)), dma((count,)), dma((count,)), dma,
        ],
        compiler_params=pltpu.CompilerParams(
            collective_id=0, has_side_effects=True, vmem_limit_bytes=(64 << 20) - (176 << 10)
        ),
    )(
        ancestors, carried, states, noise, observed, inv_var,
        jnp.transpose(psf_bank, (2, 3, 0, 1)), psf_ids.T,
        jnp.transpose(stem_w1, (1, 2, 3, 0)), stem_b1.reshape(1, channels), jnp.transpose(stem_w2, (2, 3, 0, 1)),
        stem_b2.reshape(1, channels), head_w,
    )
    return pl.pallas_call(
        deliver_kernel,
        out_shape=(pltpu.HBM(states.shape, f32), pltpu.HBM((1,), f32)),
        in_specs=[vmem] * 2,
        out_specs=(hbm, hbm),
        scratch_shapes=[pltpu.VMEM((1,), f32), dma((2,))],
        compiler_params=pltpu.CompilerParams(vmem_limit_bytes=1 << 20),
    )(next_states, log_weight)


def solution(mesh):
    return jax.shard_map(
        functools.partial(local, mesh.shape["space"], mesh.shape["particle"]),
        mesh=mesh,
        in_specs=(
            P(("tiles", "particle"), None, "space", None),
            P(("tiles", "particle"), None, "space", None),
            P("tiles", "space", None),
            P("tiles", "space", None),
            P("tiles", None, None, None),
            P(("tiles", "space"), None),
            P(("tiles", "particle"), "space"),
            P(("tiles", "particle")),
            P(),
            P(),
            P(),
            P(),
            P(),
        ),
        out_specs=(P(("tiles", "particle"), None, "space", None), P(("tiles", "particle"))),
        check_vma=False,
    )
```

```python
import functools
import math

import jax
import jax.numpy as jnp
from jax import lax
from jax.experimental import pallas as pl
from jax.experimental.pallas import tpu as pltpu
from jax.sharding import PartitionSpec as P

ALPHA_ROOT = 0.8
NOISE_ROOT = 0.6
GUIDE = 0.5
SPREAD = 0.3

MESH = pl.DeviceIdType.MESH
LANES = 128


def silu(x):
    half = 0.5 * x
    return half + half * jnp.tanh(half)


def shifted(x, step):
    if step == 0:
        return x
    axis = x.ndim - 1
    cols = x.shape[axis]
    lane = lax.broadcasted_iota(jnp.int32, x.shape, axis)
    moved = pltpu.roll(x, (-step) % cols, axis)
    keep = lane < cols - step if step > 0 else lane >= -step
    return jnp.where(keep, moved, 0.0)


def each(low, high, body):
    if high - low <= 16:
        for index in range(low, high):
            body(index)
    else:
        lax.fori_loop(low, high, lambda index, carry: (body(index), carry)[1], 0)


def step_kernel(
    strips, parts,
    anc_hbm, carried_hbm, states_hbm, noise_hbm, obs_hbm, iv_hbm, psf_hbm, ids_hbm,
    w1_hbm, b1_hbm, w2_hbm, b2_hbm, head_hbm,
    out_ref, logw_ref,
    anc_ref, carried_ref, states_ref, noise_ref, obs_ref, iv_ref, psf_ref,
    w1_ref, b1_ref, w2_ref, b2_ref, head_ref, w1t, w1k, in_sem, head2, padded,
    hi_g, lo_g, edge_s, edge_h, est_s, est_h, obs_h, iv_h, ids_h, ids_s, packs,
    xc, lo_rows, feats, w2s, corr, shifts, table, resid, obs_t, iv_t, bias,
    hi_send, hi_recv, lo_send, lo_recv, halo_send, halo_recv, pack_send, pack_recv, own_sem,
):
    bands, rows, cols = obs_ref.shape
    blocks = cols // LANES
    total = bands * rows
    channels = head_ref.shape[1]
    s = lax.axis_index("space")
    p = lax.axis_index("particle")
    me = s * parts + p
    count = strips * parts
    has_low = s > 0
    has_high = s < strips - 1

    fetches = [
        pltpu.make_async_copy(src, dst, in_sem.at[at])
        for at, (src, dst) in enumerate((
            (states_hbm, states_ref), (w1_hbm, w1_ref), (psf_hbm, psf_ref), (b1_hbm, b1_ref),
            (b2_hbm, b2_ref), (w2_hbm, w2_ref), (head_hbm, head_ref), (anc_hbm, anc_ref),
            (carried_hbm, carried_ref), (obs_hbm, obs_ref), (iv_hbm, iv_ref),
            (ids_hbm, ids_h.at[2]), (noise_hbm, noise_ref),
        ))
    ]
    for fetch in fetches:
        fetch.start()

    barrier = pltpu.get_barrier_semaphore()

    def wrapped(at, size):
        return jnp.where(at >= size, at - size, at)

    def ahead(k):
        return wrapped(s + k // parts, strips), wrapped(p + k % parts, parts)

    def behind(k):
        return wrapped(s + (strips - k // parts), strips), wrapped(p + (parts - k % parts), parts)

    def greet(k):
        ts, tp = ahead(k)
        pl.semaphore_signal(
            barrier, inc=1, device_id={"space": ts, "particle": tp}, device_id_type=MESH
        )

    each(1, count, greet)

    fetches[0].wait()
    state = states_ref[0].reshape(total, cols)
    high_part = state.astype(jnp.bfloat16)
    hi_g[p] = high_part
    lo_g[p] = (state - high_part.astype(jnp.float32)).astype(jnp.bfloat16)
    pl.semaphore_wait(barrier, count - 1)

    def gather_copy(buf, send, recv, k):
        return pltpu.make_async_remote_copy(
            src_ref=buf.at[p], dst_ref=buf.at[p],
            send_sem=send.at[k], recv_sem=recv.at[p],
            device_id={"particle": lax.rem(p + k, parts)}, device_id_type=MESH,
        )

    def gather_arrival(buf, send, recv, k):
        q = lax.rem(p + parts - k, parts)
        return pltpu.make_async_remote_copy(
            src_ref=buf.at[q], dst_ref=buf.at[q],
            send_sem=send.at[k], recv_sem=recv.at[q],
            device_id={"particle": q}, device_id_type=MESH,
        )

    for k in range(1, parts):
        gather_copy(hi_g, hi_send, hi_recv, k).start()

    def halo(kind, src, dst, side):
        towards = s + 1 if side == 0 else s - 1
        return pltpu.make_async_remote_copy(
            src_ref=src[side], dst_ref=dst.at[side],
            send_sem=halo_send.at[kind, side], recv_sem=halo_recv.at[kind, side],
            device_id={"space": towards}, device_id_type=MESH,
        )

    def start_halo(kind, src, dst):
        @pl.when(has_high)
        def _():
            halo(kind, src, dst, 0).start()

        @pl.when(has_low)
        def _():
            halo(kind, src, dst, 1).start()

    def await_halo(kind, src, dst):
        @pl.when(has_low)
        def _():
            halo(kind, src, dst, 0).wait_recv()

        @pl.when(has_high)
        def _():
            halo(kind, src, dst, 1).wait_recv()

    def end_halo(kind, src, dst):
        @pl.when(has_high)
        def _():
            halo(kind, src, dst, 0).wait_send()

        @pl.when(has_low)
        def _():
            halo(kind, src, dst, 1).wait_send()

    edge_src = (edge_s.at[0], edge_s.at[1])
    est_src = (est_s.at[0], est_s.at[1])

    def blank(buf, side):
        buf[side] = jnp.zeros(buf.shape[1:], buf.dtype)

    for buf in (edge_h, est_h, obs_h, iv_h, ids_h):
        @pl.when(jnp.logical_not(has_low))
        def _():
            blank(buf, 0)

        @pl.when(jnp.logical_not(has_high))
        def _():
            blank(buf, 1)

    for fetch in fetches[1:]:
        fetch.wait()
    start_halo(4, (ids_h.at[2],) * 2, ids_h)
    start_halo(2, (obs_ref,) * 2, obs_h)
    start_halo(3, (iv_ref,) * 2, iv_h)
    w1t[...] = jnp.zeros(w1t.shape, jnp.float32)
    for band in range(bands):
        for dy in range(3):
            for dx in range(3):
                line = w1_ref[band, dy, dx:dx + 1, :].astype(jnp.float32)
                for half in range(2):
                    at = (dy + half) * 24 + dx * 8 + band
                    w1t[at:at + 1, half * channels:(half + 1) * channels] = line
    w1k[...] = w1t[...].astype(jnp.bfloat16)
    w2s[...] = jnp.zeros(w2s.shape, jnp.bfloat16)
    for dy in range(3):
        for dx in range(3):
            block = w2_ref[dy, dx].T
            for half in range(2):
                at = ((dy + half) * 3 + dx) * channels
                w2s[at:at + channels, half * channels:(half + 1) * channels] = block
    head2[...] = jnp.zeros(head2.shape, jnp.float32)
    for half in range(2):
        head2[half * 8:half * 8 + bands, half * channels:(half + 1) * channels] = head_ref[...].astype(jnp.float32)
        bias[0:1, half * channels:(half + 1) * channels] = b1_ref[...]
        bias[1:2, half * channels:(half + 1) * channels] = b2_ref[...]
    for half in range(2):
        padded[half, 0:8] = jnp.zeros((8, channels), jnp.float32)
        padded[half, 8 + cols:16 + cols] = jnp.zeros((8, channels), jnp.float32)
    bank = psf_ref[...]
    taps, kinds = bank.shape[0] * bank.shape[1], bank.shape[2]
    flat = bank.reshape(taps * kinds, bands)
    eye = (
        lax.broadcasted_iota(jnp.int32, (8, bands), 0)
        == lax.broadcasted_iota(jnp.int32, (8, bands), 1)
    ).astype(jnp.float32)
    columns = lax.dot_general(
        eye, flat, (((1,), (1,)), ((), ())),
        precision=lax.Precision.HIGHEST, preferred_element_type=jnp.float32,
    )
    for tap in range(taps):
        for kind in range(kinds):
            at = tap * kinds + kind
            table[kind, tap] = jnp.broadcast_to(columns[:, at:at + 1], (8, LANES))
    corr[...] = jnp.zeros(corr.shape, jnp.float32)
    obs_t[...] = jnp.zeros(obs_t.shape, jnp.float32)
    iv_t[...] = jnp.zeros(iv_t.shape, jnp.float32)
    lo_rows[...] = jnp.zeros(lo_rows.shape, jnp.float32)
    xc[...] = jnp.zeros(xc.shape, jnp.float32)

    def turned(x):
        return jnp.transpose(x, (1, 0, 2))

    def rows_of(flat_part):
        return turned(flat_part.astype(jnp.float32).reshape(bands, rows, cols))

    def fill_inputs(slot, part):
        value = rows_of(part)
        base = slot * rows
        for dx in range(3):
            xc[base:base + rows, dx * 8:dx * 8 + bands, :] = shifted(value, dx - 1)

    def first_layer(i, masks):
        window = xc[pl.ds(i - 1, 4)].reshape(96, cols).astype(jnp.bfloat16)
        mixed = lax.dot_general(
            window, w1k[...], (((0,), (0,)), ((), ())), preferred_element_type=jnp.float32
        )
        value = silu(mixed + bias[0:1, :])
        for half in range(2):
            part = value[:, half * channels:(half + 1) * channels]
            if masks[half] is not None:
                part = jnp.where(masks[half], part, 0.0)
            padded[half, 8:8 + cols] = part
            at = (i - 7 + half) * cols
            for dx in range(3):
                feats[at:at + cols, dx * channels:(dx + 1) * channels] = (
                    padded[half, 7 + dx:7 + dx + cols].astype(jnp.bfloat16)
                )

    def second_layer(outs):
        window = jnp.concatenate([
            jnp.concatenate([feats[(e - 4 + r) * cols:(e - 3 + r) * cols, :] for r in range(4)], axis=1)
            for e in outs
        ], axis=0)
        mixed = jnp.dot(window, w2s[...], preferred_element_type=jnp.float32)
        hidden = silu(mixed + bias[1:2, :]).astype(jnp.bfloat16)
        both = lax.dot_general(
            head2[...].astype(jnp.bfloat16), hidden, (((1,), (1,)), ((), ())),
            preferred_element_type=jnp.float32,
        )
        for at, e in enumerate(outs):
            corr[e:e + 2] = both[:, at * cols:(at + 1) * cols].reshape(2, 8, cols)

    for k in range(1, parts):
        gather_arrival(hi_g, hi_send, hi_recv, k).wait_recv()
    ancestor = anc_ref[0, 0]
    picked_hi = hi_g[ancestor]
    fill_inputs(1, picked_hi)
    edge_s[0] = xc[14:16, 8:16, :].reshape(16, cols).astype(jnp.bfloat16)
    edge_s[1] = xc[8:10, 8:16, :].reshape(16, cols).astype(jnp.bfloat16)
    start_halo(0, edge_src, edge_h)
    for k in range(1, parts):
        gather_copy(lo_g, lo_send, lo_recv, k).start()
    for i in (9, 11, 13):
        first_layer(i, (None, None))

    second_layer((6, 8))
    await_halo(0, edge_src, edge_h)
    for side, base in ((0, 6), (1, 16)):
        value = edge_h[side].astype(jnp.float32).reshape(2, 8, cols)
        for dx in range(3):
            xc[base:base + 2, dx * 8:dx * 8 + 8, :] = shifted(value, dx - 1)
    first_layer(7, (has_low, None))
    first_layer(15, (None, has_high))
    second_layer((4, 10))

    def rough(e):
        return (xc[e + 4, 8:16, :] - NOISE_ROOT * corr[e]) / ALPHA_ROOT

    for side, base in ((0, 8), (1, 4)):
        est_s[side] = jnp.concatenate([rough(base + r) for r in range(4)], axis=0).astype(jnp.bfloat16)
    start_halo(1, est_src, est_h)

    for k in range(1, parts):
        gather_arrival(lo_g, lo_send, lo_recv, k).wait_recv()
    lo_rows[rows:2 * rows, 0:bands, :] = rows_of(lo_g[ancestor])
    await_halo(4, (ids_h.at[2],) * 2, ids_h)
    ids_copy = pltpu.make_async_copy(ids_h, ids_s, own_sem)
    ids_copy.start()
    await_halo(2, (obs_ref,) * 2, obs_h)
    await_halo(3, (iv_ref,) * 2, iv_h)
    for held, halo_buf, own in ((obs_t, obs_h, obs_ref), (iv_t, iv_h, iv_ref)):
        held[0:2, 0:bands, :] = turned(halo_buf[0])[rows - 2:rows]
        held[2:2 + rows, 0:bands, :] = turned(own[...])
        held[2 + rows:4 + rows, 0:bands, :] = turned(halo_buf[1])[0:2]

    def spread_row(e, value):
        for dx in range(5):
            shifts[e, dx] = shifted(value, dx - 2)

    def estimate_row(e):
        current = xc[e + 4, 8:16, :] + lo_rows[e + 4]
        spread_row(e, (current - NOISE_ROOT * corr[e]) / ALPHA_ROOT)

    def kind_of(q, j):
        low, high = q < 2, q >= 2 + rows
        slot = jnp.where(low, 0, jnp.where(high, 1, 2))
        row = jnp.where(low, rows - 2 + q, jnp.where(high, q - 2 - rows, q - 2))
        return ids_s[slot, j, row]

    def residual_row(q):
        for j in range(blocks):
            kind = kind_of(q, j)
            lanes = slice(j * LANES, (j + 1) * LANES)
            sums = []
            for dy in range(5):
                term = None
                for dx in range(5):
                    product = table[kind, dy * 5 + dx] * shifts[q + dy, dx, :, lanes]
                    term = product if term is None else term + product
                sums.append(term)
            blurred = sums[0] + sums[1] + sums[2] + sums[3] + sums[4]
            misfit = obs_t[q, :, lanes] - blurred
            residual = iv_t[q, :, lanes] * misfit
            if q < 2:
                residual = jnp.where(has_low, residual, 0.0)
            if q >= 2 + rows:
                residual = jnp.where(has_high, residual, 0.0)
            resid[q, :, lanes] = residual
            obs_t[q, :, lanes] = residual * misfit

    for e in range(4, 12):
        estimate_row(e)
    ids_copy.wait()
    for q in range(4, 8):
        residual_row(q)
    await_halo(1, est_src, est_h)
    for side, base in ((0, 0), (1, 12)):
        for r in range(4):
            spread_row(base + r, est_h[side, r * 8:r * 8 + 8, :].astype(jnp.float32))
    for q in (0, 1, 2, 3, 8, 9, 10, 11):
        residual_row(q)

    def adjoint(y, twist):
        moved = []
        for dx in range(5):
            pieces = []
            for j in range(blocks):
                lanes = slice(j * LANES, (j + 1) * LANES)
                term = None
                for dy in range(5):
                    q = y + 4 - dy
                    product = table[kind_of(q, j), dy * 5 + dx] * resid[q, :, lanes]
                    term = product if term is None else term + product
                pieces.append(term)
            moved.append(shifted(jnp.concatenate(pieces, axis=1), 2 - dx))
        gradient = moved[0] + moved[1] + moved[2] + moved[3] + moved[4]
        corr[y] = shifts[y + 4, 2] + GUIDE * gradient
        return twist + gradient * gradient

    twist = lax.fori_loop(0, rows, adjoint, jnp.zeros((8, cols), jnp.float32), unroll=2)
    energy = jnp.sum(obs_t[2:2 + rows], axis=0)
    mixed = -0.5 * energy + (0.5 * GUIDE) * twist
    partial = jnp.sum(mixed, axis=(0, 1), keepdims=True)
    temper = 1.0 / math.sqrt(bands * rows * strips * cols)
    prior = jnp.where(has_low, 0.0, carried_ref[0])
    packs[me] = jnp.broadcast_to(partial * temper, (1, LANES)) + prior

    def pack_copy(k):
        ts, tp = ahead(k)
        return pltpu.make_async_remote_copy(
            src_ref=packs.at[me], dst_ref=packs.at[me],
            send_sem=pack_send.at[k], recv_sem=pack_recv.at[me],
            device_id={"space": ts, "particle": tp}, device_id_type=MESH,
        )

    def pack_arrival(k):
        ts, tp = behind(k)
        t = ts * parts + tp
        return pltpu.make_async_remote_copy(
            src_ref=packs.at[t], dst_ref=packs.at[t],
            send_sem=pack_send.at[k], recv_sem=pack_recv.at[t],
            device_id={"space": ts, "particle": tp}, device_id_type=MESH,
        )

    each(1, count, lambda k: pack_copy(k).start())

    moved = turned(corr[0:rows])
    out_ref[0] = moved[0:bands] + SPREAD * noise_ref[0]

    for k in range(1, parts):
        gather_copy(hi_g, hi_send, hi_recv, k).wait_send()
        gather_copy(lo_g, lo_send, lo_recv, k).wait_send()
    end_halo(0, edge_src, edge_h)
    end_halo(1, est_src, est_h)
    end_halo(2, (obs_ref,) * 2, obs_h)
    end_halo(3, (iv_ref,) * 2, iv_h)
    end_halo(4, (ids_h.at[2],) * 2, ids_h)

    each(1, count, lambda k: pack_arrival(k).wait_recv())
    raw = packs[0:parts]
    mine = packs[p]
    for strip in range(1, strips):
        raw = raw + packs[strip * parts:(strip + 1) * parts]
        mine = mine + packs[strip * parts + p]
    highest = jnp.max(raw, axis=0)
    summed = jnp.sum(jnp.exp(raw - highest[None]), axis=0)
    logw_ref[...] = (mine - highest - jnp.log(summed))[0:1, 0:1]
    each(1, count, lambda k: pack_copy(k).wait_send())


def deliver_kernel(moved_ref, logw_ref, out_hbm, logw_hbm, logw_line, sem):
    states_copy = pltpu.make_async_copy(moved_ref, out_hbm, sem.at[0])
    states_copy.start()
    logw_line[...] = logw_ref[0, 0:1]
    logw_copy = pltpu.make_async_copy(logw_line, logw_hbm, sem.at[1])
    logw_copy.start()
    states_copy.wait()
    logw_copy.wait()


def local(
    strips, parts,
    states, noise, observed, inv_var, psf_bank, psf_ids, ancestors, carried,
    stem_w1, stem_b1, stem_w2, stem_b2, head_w,
):
    bands, rows, cols = observed.shape
    channels = stem_w1.shape[0]
    kinds = psf_bank.shape[0]
    count = strips * parts
    flat = (bands * rows, cols)
    vmem = pl.BlockSpec(memory_space=pltpu.VMEM)
    hbm = pl.BlockSpec(memory_space=pltpu.HBM)
    bf, f32 = jnp.bfloat16, jnp.float32
    dma = pltpu.SemaphoreType.DMA
    next_states, log_weight = pl.pallas_call(
        functools.partial(step_kernel, strips, parts),
        out_shape=(
            pltpu.VMEM(states.shape, f32),
            pltpu.VMEM((1, 1), f32),
        ),
        in_specs=[hbm] * 13,
        out_specs=(vmem, vmem),
        scratch_shapes=[
            pltpu.SMEM((1, 1), jnp.int32),
            pltpu.SMEM((1,), f32),
            pltpu.VMEM(states.shape, f32),
            pltpu.VMEM(states.shape, f32),
            pltpu.VMEM(observed.shape, f32),
            pltpu.VMEM(observed.shape, f32),
            pltpu.VMEM((5, 5, kinds, bands), f32),
            pltpu.VMEM((bands, 3, 3, channels), bf),
            pltpu.VMEM((1, channels), f32),
            pltpu.VMEM((3, 3, channels, channels), bf),
            pltpu.VMEM((1, channels), f32),
            pltpu.VMEM((bands, channels), bf),
            pltpu.VMEM((96, 2 * channels), f32),
            pltpu.VMEM((96, 2 * channels), bf),
            dma((13,)),
            pltpu.VMEM((16, 2 * channels), f32),
            pltpu.VMEM((2, cols + 16, channels), f32),
            pltpu.VMEM((parts,) + flat, bf),
            pltpu.VMEM((parts,) + flat, bf),
            pltpu.VMEM((2, 16, cols), bf),
            pltpu.VMEM((2, 16, cols), bf),
            pltpu.VMEM((2, 32, cols), bf),
            pltpu.VMEM((2, 32, cols), bf),
            pltpu.VMEM((2, bands, rows, cols), f32),
            pltpu.VMEM((2, bands, rows, cols), f32),
            pltpu.VMEM((3, psf_ids.shape[1], rows), jnp.int32),
            pltpu.SMEM((3, psf_ids.shape[1], rows), jnp.int32),
            pltpu.VMEM((count, 1, LANES), f32),
            pltpu.VMEM((3 * rows, 24, cols), f32),
            pltpu.VMEM((3 * rows, 8, cols), f32),
            pltpu.VMEM((10 * cols, 3 * channels), bf),
            pltpu.VMEM((12 * channels, 2 * channels), bf),
            pltpu.VMEM((16, 8, cols), f32),
            pltpu.VMEM((16, 5, 8, cols), f32),
            pltpu.VMEM((kinds, 25, 8, LANES), f32),
            pltpu.VMEM((rows + 4, 8, cols), f32),
            pltpu.VMEM((rows + 4, 8, cols), f32),
            pltpu.VMEM((rows + 4, 8, cols), f32),
            pltpu.VMEM((2, 2 * channels), f32),
            dma((parts,)), dma((parts,)), dma((parts,)), dma((parts,)),
            dma((5, 2)), dma((5, 2)), dma((count,)), dma((count,)), dma,
        ],
        compiler_params=pltpu.CompilerParams(
            collective_id=0, has_side_effects=True, vmem_limit_bytes=(64 << 20) - (176 << 10)
        ),
    )(
        ancestors, carried, states, noise, observed, inv_var,
        jnp.transpose(psf_bank, (2, 3, 0, 1)), psf_ids.T,
        jnp.transpose(stem_w1, (1, 2, 3, 0)), stem_b1.reshape(1, channels), jnp.transpose(stem_w2, (2, 3, 0, 1)),
        stem_b2.reshape(1, channels), head_w,
    )
    return pl.pallas_call(
        deliver_kernel,
        out_shape=(pltpu.HBM(states.shape, f32), pltpu.HBM((1,), f32)),
        in_specs=[vmem] * 2,
        out_specs=(hbm, hbm),
        scratch_shapes=[pltpu.VMEM((1,), f32), dma((2,))],
        compiler_params=pltpu.CompilerParams(vmem_limit_bytes=1 << 20),
    )(next_states, log_weight)


def solution(mesh):
    return jax.shard_map(
        functools.partial(local, mesh.shape["space"], mesh.shape["particle"]),
        mesh=mesh,
        in_specs=(
            P(("tiles", "particle"), None, "space", None),
            P(("tiles", "particle"), None, "space", None),
            P("tiles", "space", None),
            P("tiles", "space", None),
            P("tiles", None, None, None),
            P(("tiles", "space"), None),
            P(("tiles", "particle"), "space"),
            P(("tiles", "particle")),
            P(),
            P(),
            P(),
            P(),
            P(),
        ),
        out_specs=(P(("tiles", "particle"), None, "space", None), P(("tiles", "particle"))),
        check_vma=False,
    )
```

```python
import functools
import math

import jax
import jax.numpy as jnp
from jax import lax
from jax.experimental import pallas as pl
from jax.experimental.pallas import tpu as pltpu
from jax.sharding import PartitionSpec as P

ALPHA_ROOT = 0.8
NOISE_ROOT = 0.6
GUIDE = 0.5
SPREAD = 0.3

MESH = pl.DeviceIdType.MESH
LANES = 128


def silu(x):
    half = 0.5 * x
    return half + half * jnp.tanh(half)


def shifted(x, step):
    if step == 0:
        return x
    axis = x.ndim - 1
    cols = x.shape[axis]
    lane = lax.broadcasted_iota(jnp.int32, x.shape, axis)
    moved = pltpu.roll(x, (-step) % cols, axis)
    keep = lane < cols - step if step > 0 else lane >= -step
    return jnp.where(keep, moved, 0.0)


def each(low, high, body):
    if high - low <= 16:
        for index in range(low, high):
            body(index)
    else:
        lax.fori_loop(low, high, lambda index, carry: (body(index), carry)[1], 0)


def step_kernel(
    strips, parts,
    anc_hbm, carried_hbm, states_hbm, noise_hbm, obs_hbm, iv_hbm, psf_hbm, ids_hbm,
    w1_hbm, b1_hbm, w2_hbm, b2_hbm, head_hbm,
    out_ref, logw_ref,
    anc_ref, carried_ref, states_ref, noise_ref, obs_ref, iv_ref, psf_ref,
    w1_ref, b1_ref, w2_ref, b2_ref, head_ref, w1t, w1k, in_sem, head2, padded,
    hi_g, lo_g, edge_s, edge_h, est_s, est_h, obs_h, iv_h, ids_h, ids_s, packs,
    xc, lo_rows, feats, w2s, corr, shifts, table, resid, obs_t, iv_t, bias,
    hi_send, hi_recv, lo_send, lo_recv, halo_send, halo_recv, pack_send, pack_recv, own_sem,
):
    bands, rows, cols = obs_ref.shape
    blocks = cols // LANES
    total = bands * rows
    channels = head_ref.shape[1]
    s = lax.axis_index("space")
    p = lax.axis_index("particle")
    me = s * parts + p
    count = strips * parts
    has_low = s > 0
    has_high = s < strips - 1

    fetches = [
        pltpu.make_async_copy(src, dst, in_sem.at[at])
        for at, (src, dst) in enumerate((
            (states_hbm, states_ref), (w1_hbm, w1_ref), (psf_hbm, psf_ref), (b1_hbm, b1_ref),
            (b2_hbm, b2_ref), (w2_hbm, w2_ref), (head_hbm, head_ref), (anc_hbm, anc_ref),
            (carried_hbm, carried_ref), (obs_hbm, obs_ref), (iv_hbm, iv_ref),
            (ids_hbm, ids_h.at[2]), (noise_hbm, noise_ref),
        ))
    ]
    fetches[0].start()

    barrier = pltpu.get_barrier_semaphore()

    def wrapped(at, size):
        return jnp.where(at >= size, at - size, at)

    def ahead(k):
        return wrapped(s + k // parts, strips), wrapped(p + k % parts, parts)

    def behind(k):
        return wrapped(s + (strips - k // parts), strips), wrapped(p + (parts - k % parts), parts)

    def greet(k):
        ts, tp = ahead(k)
        pl.semaphore_signal(
            barrier, inc=1, device_id={"space": ts, "particle": tp}, device_id_type=MESH
        )

    each(1, count, greet)
    for fetch in fetches[1:]:
        fetch.start()

    fetches[0].wait()
    state = states_ref[0].reshape(total, cols)
    high_part = state.astype(jnp.bfloat16)
    hi_g[p] = high_part
    lo_g[p] = (state - high_part.astype(jnp.float32)).astype(jnp.bfloat16)
    pl.semaphore_wait(barrier, count - 1)

    def gather_copy(buf, send, recv, q):
        return pltpu.make_async_remote_copy(
            src_ref=buf.at[p], dst_ref=buf.at[p],
            send_sem=send.at[q], recv_sem=recv.at[p],
            device_id={"particle": q}, device_id_type=MESH,
        )

    def gather_arrival(buf, send, recv, q):
        return pltpu.make_async_remote_copy(
            src_ref=buf.at[q], dst_ref=buf.at[q],
            send_sem=send.at[q], recv_sem=recv.at[q],
            device_id={"particle": q}, device_id_type=MESH,
        )

    def each_other(act):
        for i in range(parts):
            q = jnp.where(p < parts // 2, parts - 1 - i, i)

            @pl.when(p != q)
            def _():
                act(q)

    each_other(lambda q: gather_copy(hi_g, hi_send, hi_recv, q).start())

    def halo(kind, src, dst, side):
        towards = s + 1 if side == 0 else s - 1
        return pltpu.make_async_remote_copy(
            src_ref=src[side], dst_ref=dst.at[side],
            send_sem=halo_send.at[kind, side], recv_sem=halo_recv.at[kind, side],
            device_id={"space": towards}, device_id_type=MESH,
        )

    def start_halo(kind, src, dst):
        @pl.when(has_high)
        def _():
            halo(kind, src, dst, 0).start()

        @pl.when(has_low)
        def _():
            halo(kind, src, dst, 1).start()

    def await_halo(kind, src, dst):
        @pl.when(has_low)
        def _():
            halo(kind, src, dst, 0).wait_recv()

        @pl.when(has_high)
        def _():
            halo(kind, src, dst, 1).wait_recv()

    def end_halo(kind, src, dst):
        @pl.when(has_high)
        def _():
            halo(kind, src, dst, 0).wait_send()

        @pl.when(has_low)
        def _():
            halo(kind, src, dst, 1).wait_send()

    edge_src = (edge_s.at[0], edge_s.at[1])
    est_src = (est_s.at[0], est_s.at[1])

    def blank(buf, side):
        buf[side] = jnp.zeros(buf.shape[1:], buf.dtype)

    for buf in (edge_h, est_h, obs_h, iv_h, ids_h):
        @pl.when(jnp.logical_not(has_low))
        def _():
            blank(buf, 0)

        @pl.when(jnp.logical_not(has_high))
        def _():
            blank(buf, 1)

    for fetch in fetches[1:]:
        fetch.wait()
    start_halo(4, (ids_h.at[2],) * 2, ids_h)
    start_halo(2, (obs_ref,) * 2, obs_h)
    start_halo(3, (iv_ref,) * 2, iv_h)
    w1t[...] = jnp.zeros(w1t.shape, jnp.float32)
    for band in range(bands):
        for dy in range(3):
            for dx in range(3):
                line = w1_ref[band, dy, dx:dx + 1, :].astype(jnp.float32)
                for half in range(2):
                    at = (dy + half) * 24 + dx * 8 + band
                    w1t[at:at + 1, half * channels:(half + 1) * channels] = line
    w1k[...] = w1t[...].astype(jnp.bfloat16)
    w2s[...] = jnp.zeros(w2s.shape, jnp.bfloat16)
    for dy in range(3):
        for dx in range(3):
            block = w2_ref[dy, dx].T
            for half in range(2):
                at = ((dy + half) * 3 + dx) * channels
                w2s[at:at + channels, half * channels:(half + 1) * channels] = block
    head2[...] = jnp.zeros(head2.shape, jnp.float32)
    for half in range(2):
        head2[half * 8:half * 8 + bands, half * channels:(half + 1) * channels] = head_ref[...].astype(jnp.float32)
        bias[0:1, half * channels:(half + 1) * channels] = b1_ref[...]
        bias[1:2, half * channels:(half + 1) * channels] = b2_ref[...]
    for half in range(2):
        padded[half, 0:8] = jnp.zeros((8, channels), jnp.float32)
        padded[half, 8 + cols:16 + cols] = jnp.zeros((8, channels), jnp.float32)
    bank = psf_ref[...]
    taps, kinds = bank.shape[0] * bank.shape[1], bank.shape[2]
    flat = bank.reshape(taps * kinds, bands)
    eye = (
        lax.broadcasted_iota(jnp.int32, (8, bands), 0)
        == lax.broadcasted_iota(jnp.int32, (8, bands), 1)
    ).astype(jnp.float32)
    columns = lax.dot_general(
        eye, flat, (((1,), (1,)), ((), ())),
        precision=lax.Precision.HIGHEST, preferred_element_type=jnp.float32,
    )
    for tap in range(taps):
        for kind in range(kinds):
            at = tap * kinds + kind
            table[kind, tap] = jnp.broadcast_to(columns[:, at:at + 1], (8, LANES))
    corr[...] = jnp.zeros(corr.shape, jnp.float32)
    obs_t[...] = jnp.zeros(obs_t.shape, jnp.float32)
    iv_t[...] = jnp.zeros(iv_t.shape, jnp.float32)
    lo_rows[...] = jnp.zeros(lo_rows.shape, jnp.float32)
    xc[...] = jnp.zeros(xc.shape, jnp.float32)

    def turned(x):
        return jnp.transpose(x, (1, 0, 2))

    def rows_of(flat_part):
        return turned(flat_part.astype(jnp.float32).reshape(bands, rows, cols))

    def fill_inputs(slot, part):
        value = rows_of(part)
        base = slot * rows
        for dx in range(3):
            xc[base:base + rows, dx * 8:dx * 8 + bands, :] = shifted(value, dx - 1)

    def first_layer(i, masks):
        window = xc[pl.ds(i - 1, 4)].reshape(96, cols).astype(jnp.bfloat16)
        mixed = lax.dot_general(
            window, w1k[...], (((0,), (0,)), ((), ())), preferred_element_type=jnp.float32
        )
        value = silu(mixed + bias[0:1, :])
        for half in range(2):
            part = value[:, half * channels:(half + 1) * channels]
            if masks[half] is not None:
                part = jnp.where(masks[half], part, 0.0)
            padded[half, 8:8 + cols] = part
            at = (i - 7 + half) * cols
            for dx in range(3):
                feats[at:at + cols, dx * channels:(dx + 1) * channels] = (
                    padded[half, 7 + dx:7 + dx + cols].astype(jnp.bfloat16)
                )

    def second_layer(outs):
        window = jnp.concatenate([
            jnp.concatenate([feats[(e - 4 + r) * cols:(e - 3 + r) * cols, :] for r in range(4)], axis=1)
            for e in outs
        ], axis=0)
        mixed = jnp.dot(window, w2s[...], preferred_element_type=jnp.float32)
        hidden = silu(mixed + bias[1:2, :]).astype(jnp.bfloat16)
        both = lax.dot_general(
            head2[...].astype(jnp.bfloat16), hidden, (((1,), (1,)), ((), ())),
            preferred_element_type=jnp.float32,
        )
        for at, e in enumerate(outs):
            corr[e:e + 2] = both[:, at * cols:(at + 1) * cols].reshape(2, 8, cols)

    each_other(lambda q: gather_arrival(hi_g, hi_send, hi_recv, q).wait_recv())
    ancestor = anc_ref[0, 0]
    picked_hi = hi_g[ancestor]
    fill_inputs(1, picked_hi)
    edge_s[0] = xc[14:16, 8:16, :].reshape(16, cols).astype(jnp.bfloat16)
    edge_s[1] = xc[8:10, 8:16, :].reshape(16, cols).astype(jnp.bfloat16)
    start_halo(0, edge_src, edge_h)
    each_other(lambda q: gather_copy(lo_g, lo_send, lo_recv, q).start())
    for i in (9, 11, 13):
        first_layer(i, (None, None))

    second_layer((6, 8))
    await_halo(0, edge_src, edge_h)
    for side, base in ((0, 6), (1, 16)):
        value = edge_h[side].astype(jnp.float32).reshape(2, 8, cols)
        for dx in range(3):
            xc[base:base + 2, dx * 8:dx * 8 + 8, :] = shifted(value, dx - 1)
    first_layer(7, (has_low, None))
    first_layer(15, (None, has_high))
    second_layer((4, 10))

    def rough(e):
        return (xc[e + 4, 8:16, :] - NOISE_ROOT * corr[e]) / ALPHA_ROOT

    for side, base in ((0, 8), (1, 4)):
        est_s[side] = jnp.concatenate([rough(base + r) for r in range(4)], axis=0).astype(jnp.bfloat16)
    start_halo(1, est_src, est_h)

    each_other(lambda q: gather_arrival(lo_g, lo_send, lo_recv, q).wait_recv())
    lo_rows[rows:2 * rows, 0:bands, :] = rows_of(lo_g[ancestor])
    await_halo(4, (ids_h.at[2],) * 2, ids_h)
    ids_copy = pltpu.make_async_copy(ids_h, ids_s, own_sem)
    ids_copy.start()
    await_halo(2, (obs_ref,) * 2, obs_h)
    await_halo(3, (iv_ref,) * 2, iv_h)
    for held, halo_buf, own in ((obs_t, obs_h, obs_ref), (iv_t, iv_h, iv_ref)):
        held[0:2, 0:bands, :] = turned(halo_buf[0])[rows - 2:rows]
        held[2:2 + rows, 0:bands, :] = turned(own[...])
        held[2 + rows:4 + rows, 0:bands, :] = turned(halo_buf[1])[0:2]

    def spread_row(e, value):
        for dx in range(5):
            shifts[e, dx] = shifted(value, dx - 2)

    def estimate_row(e):
        current = xc[e + 4, 8:16, :] + lo_rows[e + 4]
        spread_row(e, (current - NOISE_ROOT * corr[e]) / ALPHA_ROOT)

    def kind_of(q, j):
        low, high = q < 2, q >= 2 + rows
        slot = jnp.where(low, 0, jnp.where(high, 1, 2))
        row = jnp.where(low, rows - 2 + q, jnp.where(high, q - 2 - rows, q - 2))
        return ids_s[slot, j, row]

    def residual_row(q):
        for j in range(blocks):
            kind = kind_of(q, j)
            lanes = slice(j * LANES, (j + 1) * LANES)
            sums = []
            for dy in range(5):
                term = None
                for dx in range(5):
                    product = table[kind, dy * 5 + dx] * shifts[q + dy, dx, :, lanes]
                    term = product if term is None else term + product
                sums.append(term)
            blurred = sums[0] + sums[1] + sums[2] + sums[3] + sums[4]
            misfit = obs_t[q, :, lanes] - blurred
            residual = iv_t[q, :, lanes] * misfit
            if q < 2:
                residual = jnp.where(has_low, residual, 0.0)
            if q >= 2 + rows:
                residual = jnp.where(has_high, residual, 0.0)
            resid[q, :, lanes] = residual
            obs_t[q, :, lanes] = residual * misfit

    for e in range(4, 12):
        estimate_row(e)
    ids_copy.wait()
    for q in range(4, 8):
        residual_row(q)
    await_halo(1, est_src, est_h)
    for side, base in ((0, 0), (1, 12)):
        for r in range(4):
            spread_row(base + r, est_h[side, r * 8:r * 8 + 8, :].astype(jnp.float32))
    for q in (0, 1, 2, 3, 8, 9, 10, 11):
        residual_row(q)

    def adjoint(y, twist):
        moved = []
        for dx in range(5):
            pieces = []
            for j in range(blocks):
                lanes = slice(j * LANES, (j + 1) * LANES)
                term = None
                for dy in range(5):
                    q = y + 4 - dy
                    product = table[kind_of(q, j), dy * 5 + dx] * resid[q, :, lanes]
                    term = product if term is None else term + product
                pieces.append(term)
            moved.append(shifted(jnp.concatenate(pieces, axis=1), 2 - dx))
        gradient = moved[0] + moved[1] + moved[2] + moved[3] + moved[4]
        corr[y] = shifts[y + 4, 2] + GUIDE * gradient
        return twist + gradient * gradient

    twist = functools.reduce(lambda twist, y: adjoint(y, twist), range(rows), jnp.zeros((8, cols), jnp.float32))
    energy = jnp.sum(obs_t[2:2 + rows], axis=0)
    mixed = -0.5 * energy + (0.5 * GUIDE) * twist
    partial = jnp.sum(mixed, axis=(0, 1), keepdims=True)
    temper = 1.0 / math.sqrt(bands * rows * strips * cols)
    prior = jnp.where(has_low, 0.0, carried_ref[0])
    packs[me] = jnp.broadcast_to(partial * temper, (1, LANES)) + prior

    def pack_copy(k):
        tp, ts = k // strips, wrapped(s + k % strips, strips)
        return ts * parts + tp, pltpu.make_async_remote_copy(
            src_ref=packs.at[me], dst_ref=packs.at[me],
            send_sem=pack_send.at[k], recv_sem=pack_recv.at[me],
            device_id={"space": ts, "particle": tp}, device_id_type=MESH,
        )

    def send_pack(k):
        t, copy = pack_copy(k)

        @pl.when(t != me)
        def _():
            copy.start()

    def end_pack(k):
        t, copy = pack_copy(k)

        @pl.when(t != me)
        def _():
            copy.wait_send()

    def pack_arrival(k):
        ts, tp = behind(k)
        t = ts * parts + tp
        return pltpu.make_async_remote_copy(
            src_ref=packs.at[t], dst_ref=packs.at[t],
            send_sem=pack_send.at[k], recv_sem=pack_recv.at[t],
            device_id={"space": ts, "particle": tp}, device_id_type=MESH,
        )

    each(0, count, send_pack)

    moved = turned(corr[0:rows])
    out_ref[0] = moved[0:bands] + SPREAD * noise_ref[0]

    each_other(lambda q: gather_copy(hi_g, hi_send, hi_recv, q).wait_send())
    each_other(lambda q: gather_copy(lo_g, lo_send, lo_recv, q).wait_send())
    end_halo(0, edge_src, edge_h)
    end_halo(1, est_src, est_h)
    end_halo(2, (obs_ref,) * 2, obs_h)
    end_halo(3, (iv_ref,) * 2, iv_h)
    end_halo(4, (ids_h.at[2],) * 2, ids_h)

    each(1, count, lambda k: pack_arrival(k).wait_recv())
    raw = packs[0:parts]
    mine = packs[p]
    for strip in range(1, strips):
        raw = raw + packs[strip * parts:(strip + 1) * parts]
        mine = mine + packs[strip * parts + p]
    highest = jnp.max(raw, axis=0)
    summed = jnp.sum(jnp.exp(raw - highest[None]), axis=0)
    logw_ref[...] = (mine - highest - jnp.log(summed))[0:1, 0:1]
    each(0, count, end_pack)


def deliver_kernel(moved_ref, logw_ref, out_hbm, logw_hbm, logw_line, sem):
    states_copy = pltpu.make_async_copy(moved_ref, out_hbm, sem.at[0])
    states_copy.start()
    logw_line[...] = logw_ref[0, 0:1]
    logw_copy = pltpu.make_async_copy(logw_line, logw_hbm, sem.at[1])
    logw_copy.start()
    states_copy.wait()
    logw_copy.wait()


def local(
    strips, parts,
    states, noise, observed, inv_var, psf_bank, psf_ids, ancestors, carried,
    stem_w1, stem_b1, stem_w2, stem_b2, head_w,
):
    bands, rows, cols = observed.shape
    channels = stem_w1.shape[0]
    kinds = psf_bank.shape[0]
    count = strips * parts
    flat = (bands * rows, cols)
    vmem = pl.BlockSpec(memory_space=pltpu.VMEM)
    hbm = pl.BlockSpec(memory_space=pltpu.HBM)
    bf, f32 = jnp.bfloat16, jnp.float32
    dma = pltpu.SemaphoreType.DMA
    next_states, log_weight = pl.pallas_call(
        functools.partial(step_kernel, strips, parts),
        out_shape=(
            pltpu.VMEM(states.shape, f32),
            pltpu.VMEM((1, 1), f32),
        ),
        in_specs=[hbm] * 13,
        out_specs=(vmem, vmem),
        scratch_shapes=[
            pltpu.SMEM((1, 1), jnp.int32),
            pltpu.SMEM((1,), f32),
            pltpu.VMEM(states.shape, f32),
            pltpu.VMEM(states.shape, f32),
            pltpu.VMEM(observed.shape, f32),
            pltpu.VMEM(observed.shape, f32),
            pltpu.VMEM((5, 5, kinds, bands), f32),
            pltpu.VMEM((bands, 3, 3, channels), bf),
            pltpu.VMEM((1, channels), f32),
            pltpu.VMEM((3, 3, channels, channels), bf),
            pltpu.VMEM((1, channels), f32),
            pltpu.VMEM((bands, channels), bf),
            pltpu.VMEM((96, 2 * channels), f32),
            pltpu.VMEM((96, 2 * channels), bf),
            dma((13,)),
            pltpu.VMEM((16, 2 * channels), f32),
            pltpu.VMEM((2, cols + 16, channels), f32),
            pltpu.VMEM((parts,) + flat, bf),
            pltpu.VMEM((parts,) + flat, bf),
            pltpu.VMEM((2, 16, cols), bf),
            pltpu.VMEM((2, 16, cols), bf),
            pltpu.VMEM((2, 32, cols), bf),
            pltpu.VMEM((2, 32, cols), bf),
            pltpu.VMEM((2, bands, rows, cols), f32),
            pltpu.VMEM((2, bands, rows, cols), f32),
            pltpu.VMEM((3, psf_ids.shape[1], rows), jnp.int32),
            pltpu.SMEM((3, psf_ids.shape[1], rows), jnp.int32),
            pltpu.VMEM((count, 1, LANES), f32),
            pltpu.VMEM((3 * rows, 24, cols), f32),
            pltpu.VMEM((3 * rows, 8, cols), f32),
            pltpu.VMEM((10 * cols, 3 * channels), bf),
            pltpu.VMEM((12 * channels, 2 * channels), bf),
            pltpu.VMEM((16, 8, cols), f32),
            pltpu.VMEM((16, 5, 8, cols), f32),
            pltpu.VMEM((kinds, 25, 8, LANES), f32),
            pltpu.VMEM((rows + 4, 8, cols), f32),
            pltpu.VMEM((rows + 4, 8, cols), f32),
            pltpu.VMEM((rows + 4, 8, cols), f32),
            pltpu.VMEM((2, 2 * channels), f32),
            dma((parts,)), dma((parts,)), dma((parts,)), dma((parts,)),
            dma((5, 2)), dma((5, 2)), dma((count,)), dma((count,)), dma,
        ],
        compiler_params=pltpu.CompilerParams(
            collective_id=0, has_side_effects=True, vmem_limit_bytes=(64 << 20) - (176 << 10)
        ),
    )(
        ancestors, carried, states, noise, observed, inv_var,
        jnp.transpose(psf_bank, (2, 3, 0, 1)), psf_ids.T,
        jnp.transpose(stem_w1, (1, 2, 3, 0)), stem_b1.reshape(1, channels), jnp.transpose(stem_w2, (2, 3, 0, 1)),
        stem_b2.reshape(1, channels), head_w,
    )
    return pl.pallas_call(
        deliver_kernel,
        out_shape=(pltpu.HBM(states.shape, f32), pltpu.HBM((1,), f32)),
        in_specs=[vmem] * 2,
        out_specs=(hbm, hbm),
        scratch_shapes=[pltpu.VMEM((1,), f32), dma((2,))],
        compiler_params=pltpu.CompilerParams(vmem_limit_bytes=1 << 20),
    )(next_states, log_weight)


def solution(mesh):
    return jax.shard_map(
        functools.partial(local, mesh.shape["space"], mesh.shape["particle"]),
        mesh=mesh,
        in_specs=(
            P(("tiles", "particle"), None, "space", None),
            P(("tiles", "particle"), None, "space", None),
            P("tiles", "space", None),
            P("tiles", "space", None),
            P("tiles", None, None, None),
            P(("tiles", "space"), None),
            P(("tiles", "particle"), "space"),
            P(("tiles", "particle")),
            P(),
            P(),
            P(),
            P(),
            P(),
        ),
        out_specs=(P(("tiles", "particle"), None, "space", None), P(("tiles", "particle"))),
        check_vma=False,
    )
```

```python
import functools
import math

import jax
import jax.numpy as jnp
from jax import lax
from jax.experimental import pallas as pl
from jax.experimental.pallas import tpu as pltpu
from jax.sharding import PartitionSpec as P

ALPHA_ROOT = 0.8
NOISE_ROOT = 0.6
GUIDE = 0.5
SPREAD = 0.3

MESH = pl.DeviceIdType.MESH
LANES = 128


def silu(x):
    half = 0.5 * x
    return half + half * jnp.tanh(half)


def shifted(x, step):
    if step == 0:
        return x
    axis = x.ndim - 1
    cols = x.shape[axis]
    lane = lax.broadcasted_iota(jnp.int32, x.shape, axis)
    moved = pltpu.roll(x, (-step) % cols, axis)
    keep = lane < cols - step if step > 0 else lane >= -step
    return jnp.where(keep, moved, 0.0)


def each(low, high, body):
    if high - low <= 16:
        for index in range(low, high):
            body(index)
    else:
        lax.fori_loop(low, high, lambda index, carry: (body(index), carry)[1], 0)


def step_kernel(
    strips, parts,
    anc_hbm, carried_hbm, states_hbm, noise_hbm, obs_hbm, iv_hbm, psf_hbm, ids_hbm,
    w1_hbm, b1_hbm, w2_hbm, b2_hbm, head_hbm,
    out_ref, logw_ref,
    anc_ref, carried_ref, states_ref, noise_ref, obs_ref, iv_ref, psf_ref,
    w1_ref, b1_ref, w2_ref, b2_ref, head_ref, w1t, w1k, in_sem, head2, padded,
    hi_g, lo_g, edge_s, edge_h, est_s, est_h, obs_h, iv_h, ids_h, ids_s, packs,
    xc, lo_rows, feats, w2s, corr, shifts, table, resid, obs_t, iv_t, bias,
    hi_send, hi_recv, lo_send, lo_recv, halo_send, halo_recv, pack_send, pack_recv, own_sem,
):
    bands, rows, cols = obs_ref.shape
    blocks = cols // LANES
    total = bands * rows
    channels = head_ref.shape[1]
    s = lax.axis_index("space")
    p = lax.axis_index("particle")
    me = s * parts + p
    count = strips * parts
    has_low = s > 0
    has_high = s < strips - 1

    fetches = [
        pltpu.make_async_copy(src, dst, in_sem.at[at])
        for at, (src, dst) in enumerate((
            (states_hbm, states_ref), (w1_hbm, w1_ref), (psf_hbm, psf_ref), (b1_hbm, b1_ref),
            (b2_hbm, b2_ref), (w2_hbm, w2_ref), (head_hbm, head_ref), (anc_hbm, anc_ref),
            (carried_hbm, carried_ref), (obs_hbm, obs_ref), (iv_hbm, iv_ref),
            (ids_hbm, ids_h.at[2]), (noise_hbm, noise_ref),
        ))
    ]
    fetches[0].start()

    barrier = pltpu.get_barrier_semaphore()

    def wrapped(at, size):
        return jnp.where(at >= size, at - size, at)

    def ahead(k):
        return wrapped(s + k // parts, strips), wrapped(p + k % parts, parts)

    def behind(k):
        return wrapped(s + (strips - k // parts), strips), wrapped(p + (parts - k % parts), parts)

    def greet(k):
        ts, tp = ahead(k)
        pl.semaphore_signal(
            barrier, inc=1, device_id={"space": ts, "particle": tp}, device_id_type=MESH
        )

    each(1, count, greet)
    for fetch in fetches[1:]:
        fetch.start()

    fetches[0].wait()
    state = states_ref[0].reshape(total, cols)
    high_part = state.astype(jnp.bfloat16)
    hi_g[p] = high_part
    lo_g[p] = (state - high_part.astype(jnp.float32)).astype(jnp.bfloat16)
    pl.semaphore_wait(barrier, count - 1)

    def gather_copy(buf, send, recv, q):
        return pltpu.make_async_remote_copy(
            src_ref=buf.at[p], dst_ref=buf.at[p],
            send_sem=send.at[q], recv_sem=recv.at[p],
            device_id={"particle": q}, device_id_type=MESH,
        )

    def gather_arrival(buf, send, recv, q):
        return pltpu.make_async_remote_copy(
            src_ref=buf.at[q], dst_ref=buf.at[q],
            send_sem=send.at[q], recv_sem=recv.at[q],
            device_id={"particle": q}, device_id_type=MESH,
        )

    def each_other(act):
        for i in range(parts):
            q = jnp.where(p < parts // 2, parts - 1 - i, i)

            @pl.when(p != q)
            def _():
                act(q)

    each_other(lambda q: gather_copy(hi_g, hi_send, hi_recv, q).start())

    def halo(kind, src, dst, side):
        towards = s + 1 if side == 0 else s - 1
        return pltpu.make_async_remote_copy(
            src_ref=src[side], dst_ref=dst.at[side],
            send_sem=halo_send.at[kind, side], recv_sem=halo_recv.at[kind, side],
            device_id={"space": towards}, device_id_type=MESH,
        )

    def start_halo(kind, src, dst):
        @pl.when(has_high)
        def _():
            halo(kind, src, dst, 0).start()

        @pl.when(has_low)
        def _():
            halo(kind, src, dst, 1).start()

    def await_halo(kind, src, dst):
        @pl.when(has_low)
        def _():
            halo(kind, src, dst, 0).wait_recv()

        @pl.when(has_high)
        def _():
            halo(kind, src, dst, 1).wait_recv()

    def end_halo(kind, src, dst):
        @pl.when(has_high)
        def _():
            halo(kind, src, dst, 0).wait_send()

        @pl.when(has_low)
        def _():
            halo(kind, src, dst, 1).wait_send()

    edge_src = (edge_s.at[0], edge_s.at[1])
    est_src = (est_s.at[0], est_s.at[1])

    def blank(buf, side):
        buf[side] = jnp.zeros(buf.shape[1:], buf.dtype)

    for buf in (edge_h, est_h, obs_h, iv_h, ids_h):
        @pl.when(jnp.logical_not(has_low))
        def _():
            blank(buf, 0)

        @pl.when(jnp.logical_not(has_high))
        def _():
            blank(buf, 1)

    for fetch in fetches[1:]:
        fetch.wait()
    start_halo(4, (ids_h.at[2],) * 2, ids_h)
    start_halo(2, (obs_ref,) * 2, obs_h)
    start_halo(3, (iv_ref,) * 2, iv_h)
    w1t[...] = jnp.zeros(w1t.shape, jnp.float32)
    for band in range(bands):
        for dy in range(3):
            for dx in range(3):
                line = w1_ref[band, dy, dx:dx + 1, :].astype(jnp.float32)
                for half in range(2):
                    at = (dy + half) * 24 + dx * 8 + band
                    w1t[at:at + 1, half * channels:(half + 1) * channels] = line
    w1k[...] = w1t[...].astype(jnp.bfloat16)
    w2s[...] = jnp.zeros(w2s.shape, jnp.bfloat16)
    for dy in range(3):
        for dx in range(3):
            block = w2_ref[dy, dx].T
            for half in range(2):
                at = ((dy + half) * 3 + dx) * channels
                w2s[at:at + channels, half * channels:(half + 1) * channels] = block
    head2[...] = jnp.zeros(head2.shape, jnp.float32)
    for half in range(2):
        head2[half * 8:half * 8 + bands, half * channels:(half + 1) * channels] = head_ref[...].astype(jnp.float32)
        bias[0:1, half * channels:(half + 1) * channels] = b1_ref[...]
        bias[1:2, half * channels:(half + 1) * channels] = b2_ref[...]
    for half in range(2):
        padded[half, 0:8] = jnp.zeros((8, channels), jnp.float32)
        padded[half, 8 + cols:16 + cols] = jnp.zeros((8, channels), jnp.float32)
    bank = psf_ref[...]
    taps, kinds = bank.shape[0] * bank.shape[1], bank.shape[2]
    flat = bank.reshape(taps * kinds, bands)
    eye = (
        lax.broadcasted_iota(jnp.int32, (8, bands), 0)
        == lax.broadcasted_iota(jnp.int32, (8, bands), 1)
    ).astype(jnp.float32)
    columns = lax.dot_general(
        eye, flat, (((1,), (1,)), ((), ())),
        precision=lax.Precision.HIGHEST, preferred_element_type=jnp.float32,
    )
    for tap in range(taps):
        for kind in range(kinds):
            at = tap * kinds + kind
            table[kind, tap] = jnp.broadcast_to(columns[:, at:at + 1], (8, LANES))
    corr[...] = jnp.zeros(corr.shape, jnp.float32)
    obs_t[...] = jnp.zeros(obs_t.shape, jnp.float32)
    iv_t[...] = jnp.zeros(iv_t.shape, jnp.float32)
    lo_rows[...] = jnp.zeros(lo_rows.shape, jnp.float32)
    xc[...] = jnp.zeros(xc.shape, jnp.float32)

    def turned(x):
        return jnp.transpose(x, (1, 0, 2))

    def rows_of(flat_part):
        return turned(flat_part.astype(jnp.float32).reshape(bands, rows, cols))

    def fill_inputs(slot, part):
        value = rows_of(part)
        base = slot * rows
        for dx in range(3):
            xc[base:base + rows, dx * 8:dx * 8 + bands, :] = shifted(value, dx - 1)

    def first_layer(i, masks):
        window = xc[pl.ds(i - 1, 4)].reshape(96, cols).astype(jnp.bfloat16)
        mixed = lax.dot_general(
            window, w1k[...], (((0,), (0,)), ((), ())), preferred_element_type=jnp.float32
        )
        value = silu(mixed + bias[0:1, :])
        for half in range(2):
            part = value[:, half * channels:(half + 1) * channels]
            if masks[half] is not None:
                part = jnp.where(masks[half], part, 0.0)
            padded[half, 8:8 + cols] = part
            at = (i - 7 + half) * cols
            for dx in range(3):
                feats[at:at + cols, dx * channels:(dx + 1) * channels] = (
                    padded[half, 7 + dx:7 + dx + cols].astype(jnp.bfloat16)
                )

    def second_layer(outs):
        window = jnp.concatenate([
            jnp.concatenate([feats[(e - 4 + r) * cols:(e - 3 + r) * cols, :] for r in range(4)], axis=1)
            for e in outs
        ], axis=0)
        mixed = jnp.dot(window, w2s[...], preferred_element_type=jnp.float32)
        hidden = silu(mixed + bias[1:2, :]).astype(jnp.bfloat16)
        both = lax.dot_general(
            head2[...].astype(jnp.bfloat16), hidden, (((1,), (1,)), ((), ())),
            preferred_element_type=jnp.float32,
        )
        for at, e in enumerate(outs):
            corr[e:e + 2] = both[:, at * cols:(at + 1) * cols].reshape(2, 8, cols)

    each_other(lambda q: gather_arrival(hi_g, hi_send, hi_recv, q).wait_recv())
    ancestor = anc_ref[0, 0]
    picked_hi = hi_g[ancestor]
    fill_inputs(1, picked_hi)
    edge_s[0] = xc[14:16, 8:16, :].reshape(16, cols).astype(jnp.bfloat16)
    edge_s[1] = xc[8:10, 8:16, :].reshape(16, cols).astype(jnp.bfloat16)
    start_halo(0, edge_src, edge_h)
    each_other(lambda q: gather_copy(lo_g, lo_send, lo_recv, q).start())
    for i in (9, 11, 13):
        first_layer(i, (None, None))

    second_layer((6, 8))
    await_halo(0, edge_src, edge_h)
    for side, base in ((0, 6), (1, 16)):
        value = edge_h[side].astype(jnp.float32).reshape(2, 8, cols)
        for dx in range(3):
            xc[base:base + 2, dx * 8:dx * 8 + 8, :] = shifted(value, dx - 1)
    first_layer(7, (has_low, None))
    first_layer(15, (None, has_high))
    second_layer((4, 10))

    def rough(e):
        return (xc[e + 4, 8:16, :] - NOISE_ROOT * corr[e]) / ALPHA_ROOT

    for side, base in ((0, 8), (1, 4)):
        est_s[side] = jnp.concatenate([rough(base + r) for r in range(4)], axis=0).astype(jnp.bfloat16)
    start_halo(1, est_src, est_h)

    each_other(lambda q: gather_arrival(lo_g, lo_send, lo_recv, q).wait_recv())
    lo_rows[rows:2 * rows, 0:bands, :] = rows_of(lo_g[ancestor])
    await_halo(4, (ids_h.at[2],) * 2, ids_h)
    ids_copy = pltpu.make_async_copy(ids_h, ids_s, own_sem)
    ids_copy.start()
    await_halo(2, (obs_ref,) * 2, obs_h)
    await_halo(3, (iv_ref,) * 2, iv_h)
    for held, halo_buf, own in ((obs_t, obs_h, obs_ref), (iv_t, iv_h, iv_ref)):
        held[0:2, 0:bands, :] = turned(halo_buf[0])[rows - 2:rows]
        held[2:2 + rows, 0:bands, :] = turned(own[...])
        held[2 + rows:4 + rows, 0:bands, :] = turned(halo_buf[1])[0:2]

    def spread_row(e, value):
        for dx in range(5):
            shifts[e, dx] = shifted(value, dx - 2)

    def estimate_row(e):
        current = xc[e + 4, 8:16, :] + lo_rows[e + 4]
        spread_row(e, (current - NOISE_ROOT * corr[e]) / ALPHA_ROOT)

    def kind_of(q, j):
        low, high = q < 2, q >= 2 + rows
        slot = jnp.where(low, 0, jnp.where(high, 1, 2))
        row = jnp.where(low, rows - 2 + q, jnp.where(high, q - 2 - rows, q - 2))
        return ids_s[slot, j, row]

    def residual_row(q):
        for j in range(blocks):
            kind = kind_of(q, j)
            lanes = slice(j * LANES, (j + 1) * LANES)
            sums = []
            for dy in range(5):
                term = None
                for dx in range(5):
                    product = table[kind, dy * 5 + dx] * shifts[q + dy, dx, :, lanes]
                    term = product if term is None else term + product
                sums.append(term)
            blurred = sums[0] + sums[1] + sums[2] + sums[3] + sums[4]
            misfit = obs_t[q, :, lanes] - blurred
            residual = iv_t[q, :, lanes] * misfit
            if q < 2:
                residual = jnp.where(has_low, residual, 0.0)
            if q >= 2 + rows:
                residual = jnp.where(has_high, residual, 0.0)
            resid[q, :, lanes] = residual
            obs_t[q, :, lanes] = residual * misfit

    for e in range(4, 12):
        estimate_row(e)
    ids_copy.wait()
    for q in range(4, 8):
        residual_row(q)
    await_halo(1, est_src, est_h)
    for side, base in ((0, 0), (1, 12)):
        for r in range(4):
            spread_row(base + r, est_h[side, r * 8:r * 8 + 8, :].astype(jnp.float32))
    for q in (0, 1, 2, 3, 8, 9, 10, 11):
        residual_row(q)

    def adjoint(y, twist):
        moved = []
        for dx in range(5):
            pieces = []
            for j in range(blocks):
                lanes = slice(j * LANES, (j + 1) * LANES)
                term = None
                for dy in range(5):
                    q = y + 4 - dy
                    product = table[kind_of(q, j), dy * 5 + dx] * resid[q, :, lanes]
                    term = product if term is None else term + product
                pieces.append(term)
            moved.append(shifted(jnp.concatenate(pieces, axis=1), 2 - dx))
        gradient = moved[0] + moved[1] + moved[2] + moved[3] + moved[4]
        corr[y] = shifts[y + 4, 2] + GUIDE * gradient
        return twist + gradient * gradient

    twist = functools.reduce(lambda twist, y: adjoint(y, twist), range(rows), jnp.zeros((8, cols), jnp.float32))
    energy = jnp.sum(obs_t[2:2 + rows], axis=0)
    mixed = -0.5 * energy + (0.5 * GUIDE) * twist
    partial = jnp.sum(mixed, axis=(0, 1), keepdims=True)
    temper = 1.0 / math.sqrt(bands * rows * strips * cols)
    prior = jnp.where(has_low, 0.0, carried_ref[0])
    packs[me] = jnp.broadcast_to(partial * temper, (1, LANES)) + prior

    def pack_copy(k):
        tp, ts = k // strips, wrapped(s + k % strips, strips)
        return ts * parts + tp, pltpu.make_async_remote_copy(
            src_ref=packs.at[me], dst_ref=packs.at[me],
            send_sem=pack_send.at[k], recv_sem=pack_recv.at[me],
            device_id={"space": ts, "particle": tp}, device_id_type=MESH,
        )

    def send_pack(k):
        t, copy = pack_copy(k)

        @pl.when(t != me)
        def _():
            copy.start()

    def end_pack(k):
        t, copy = pack_copy(k)

        @pl.when(t != me)
        def _():
            copy.wait_send()

    def pack_arrival(k):
        ts, tp = behind(k)
        t = ts * parts + tp
        return pltpu.make_async_remote_copy(
            src_ref=packs.at[t], dst_ref=packs.at[t],
            send_sem=pack_send.at[k], recv_sem=pack_recv.at[t],
            device_id={"space": ts, "particle": tp}, device_id_type=MESH,
        )

    each(0, count, send_pack)

    moved = turned(corr[0:rows])
    out_ref[0] = moved[0:bands] + SPREAD * noise_ref[0]

    each_other(lambda q: gather_copy(hi_g, hi_send, hi_recv, q).wait_send())
    each_other(lambda q: gather_copy(lo_g, lo_send, lo_recv, q).wait_send())
    end_halo(0, edge_src, edge_h)
    end_halo(1, est_src, est_h)
    end_halo(2, (obs_ref,) * 2, obs_h)
    end_halo(3, (iv_ref,) * 2, iv_h)
    end_halo(4, (ids_h.at[2],) * 2, ids_h)

    each(1, count, lambda k: pack_arrival(k).wait_recv())
    raw = packs[0:parts]
    mine = packs[p]
    for strip in range(1, strips):
        raw = raw + packs[strip * parts:(strip + 1) * parts]
        mine = mine + packs[strip * parts + p]
    highest = jnp.max(raw, axis=0)
    summed = jnp.sum(jnp.exp(raw - highest[None]), axis=0)
    logw_ref[...] = jnp.broadcast_to(mine - highest - jnp.log(summed), (8, LANES))
    each(0, count, end_pack)


def deliver_kernel(moved_ref, logw_ref, out_hbm, logw_hbm, logw_line, sem):
    states_copy = pltpu.make_async_copy(moved_ref, out_hbm, sem.at[0])
    states_copy.start()
    logw_line[...] = logw_ref[0, 0:1]
    logw_copy = pltpu.make_async_copy(logw_line, logw_hbm, sem.at[1])
    logw_copy.start()
    states_copy.wait()
    logw_copy.wait()


def local(
    strips, parts,
    states, noise, observed, inv_var, psf_bank, psf_ids, ancestors, carried,
    stem_w1, stem_b1, stem_w2, stem_b2, head_w,
):
    bands, rows, cols = observed.shape
    channels = stem_w1.shape[0]
    kinds = psf_bank.shape[0]
    count = strips * parts
    flat = (bands * rows, cols)
    vmem = pl.BlockSpec(memory_space=pltpu.VMEM)
    hbm = pl.BlockSpec(memory_space=pltpu.HBM)
    bf, f32 = jnp.bfloat16, jnp.float32
    dma = pltpu.SemaphoreType.DMA
    next_states, log_weight = pl.pallas_call(
        functools.partial(step_kernel, strips, parts),
        out_shape=(
            pltpu.VMEM(states.shape, f32),
            pltpu.VMEM((8, LANES), f32),
        ),
        in_specs=[hbm] * 13,
        out_specs=(vmem, vmem),
        scratch_shapes=[
            pltpu.SMEM((1, 1), jnp.int32),
            pltpu.SMEM((1,), f32),
            pltpu.VMEM(states.shape, f32),
            pltpu.VMEM(states.shape, f32),
            pltpu.VMEM(observed.shape, f32),
            pltpu.VMEM(observed.shape, f32),
            pltpu.VMEM((5, 5, kinds, bands), f32),
            pltpu.VMEM((bands, 3, 3, channels), bf),
            pltpu.VMEM((1, channels), f32),
            pltpu.VMEM((3, 3, channels, channels), bf),
            pltpu.VMEM((1, channels), f32),
            pltpu.VMEM((bands, channels), bf),
            pltpu.VMEM((96, 2 * channels), f32),
            pltpu.VMEM((96, 2 * channels), bf),
            dma((13,)),
            pltpu.VMEM((16, 2 * channels), f32),
            pltpu.VMEM((2, cols + 16, channels), f32),
            pltpu.VMEM((parts,) + flat, bf),
            pltpu.VMEM((parts,) + flat, bf),
            pltpu.VMEM((2, 16, cols), bf),
            pltpu.VMEM((2, 16, cols), bf),
            pltpu.VMEM((2, 32, cols), bf),
            pltpu.VMEM((2, 32, cols), bf),
            pltpu.VMEM((2, bands, rows, cols), f32),
            pltpu.VMEM((2, bands, rows, cols), f32),
            pltpu.VMEM((3, psf_ids.shape[1], rows), jnp.int32),
            pltpu.SMEM((3, psf_ids.shape[1], rows), jnp.int32),
            pltpu.VMEM((count, 1, LANES), f32),
            pltpu.VMEM((3 * rows, 24, cols), f32),
            pltpu.VMEM((3 * rows, 8, cols), f32),
            pltpu.VMEM((10 * cols, 3 * channels), bf),
            pltpu.VMEM((12 * channels, 2 * channels), bf),
            pltpu.VMEM((16, 8, cols), f32),
            pltpu.VMEM((16, 5, 8, cols), f32),
            pltpu.VMEM((kinds, 25, 8, LANES), f32),
            pltpu.VMEM((rows + 4, 8, cols), f32),
            pltpu.VMEM((rows + 4, 8, cols), f32),
            pltpu.VMEM((rows + 4, 8, cols), f32),
            pltpu.VMEM((2, 2 * channels), f32),
            dma((parts,)), dma((parts,)), dma((parts,)), dma((parts,)),
            dma((5, 2)), dma((5, 2)), dma((count,)), dma((count,)), dma,
        ],
        compiler_params=pltpu.CompilerParams(
            collective_id=0, has_side_effects=True, vmem_limit_bytes=(64 << 20) - (176 << 10)
        ),
    )(
        ancestors, carried, states, noise, observed, inv_var,
        jnp.transpose(psf_bank, (2, 3, 0, 1)), psf_ids.T,
        jnp.transpose(stem_w1, (1, 2, 3, 0)), stem_b1.reshape(1, channels), jnp.transpose(stem_w2, (2, 3, 0, 1)),
        stem_b2.reshape(1, channels), head_w,
    )
    return pl.pallas_call(
        deliver_kernel,
        out_shape=(pltpu.HBM(states.shape, f32), pltpu.HBM((1,), f32)),
        in_specs=[vmem] * 2,
        out_specs=(hbm, hbm),
        scratch_shapes=[pltpu.VMEM((1,), f32), dma((2,))],
        compiler_params=pltpu.CompilerParams(vmem_limit_bytes=1 << 20),
    )(next_states, log_weight)


def solution(mesh):
    return jax.shard_map(
        functools.partial(local, mesh.shape["space"], mesh.shape["particle"]),
        mesh=mesh,
        in_specs=(
            P(("tiles", "particle"), None, "space", None),
            P(("tiles", "particle"), None, "space", None),
            P("tiles", "space", None),
            P("tiles", "space", None),
            P("tiles", None, None, None),
            P(("tiles", "space"), None),
            P(("tiles", "particle"), "space"),
            P(("tiles", "particle")),
            P(),
            P(),
            P(),
            P(),
            P(),
        ),
        out_specs=(P(("tiles", "particle"), None, "space", None), P(("tiles", "particle"))),
        check_vma=False,
    )
```

```python
import functools
import math

import jax
import jax.numpy as jnp
from jax import lax
from jax.experimental import pallas as pl
from jax.experimental.pallas import tpu as pltpu
from jax.sharding import PartitionSpec as P

ALPHA_ROOT = 0.8
NOISE_ROOT = 0.6
GUIDE = 0.5
SPREAD = 0.3

MESH = pl.DeviceIdType.MESH
LANES = 128


def silu(x):
    half = 0.5 * x
    return half + half * jnp.tanh(half)


def shifted(x, step):
    if step == 0:
        return x
    axis = x.ndim - 1
    cols = x.shape[axis]
    lane = lax.broadcasted_iota(jnp.int32, x.shape, axis)
    moved = pltpu.roll(x, (-step) % cols, axis)
    keep = lane < cols - step if step > 0 else lane >= -step
    return jnp.where(keep, moved, 0.0)


def each(low, high, body):
    if high - low <= 16:
        for index in range(low, high):
            body(index)
    else:
        lax.fori_loop(low, high, lambda index, carry: (body(index), carry)[1], 0)


def step_kernel(
    strips, parts,
    anc_hbm, carried_hbm, states_hbm, noise_hbm, obs_hbm, iv_hbm, psf_hbm, ids_hbm,
    w1_hbm, b1_hbm, w2_hbm, b2_hbm, head_hbm,
    out_ref, logw_ref,
    anc_ref, carried_ref, states_ref, noise_ref, obs_ref, iv_ref, psf_ref,
    w1_ref, b1_ref, w2_ref, b2_ref, head_ref, w1t, w1k, in_sem, head2, padded,
    hi_g, lo_g, edge_s, edge_h, est_s, est_h, obs_h, iv_h, ids_h, ids_s, packs,
    xc, lo_rows, begun, feats, w2s, corr, shifts, table, resid, obs_t, iv_t, bias,
    hi_send, hi_recv, lo_send, lo_recv, halo_send, halo_recv, pack_send, pack_recv, own_sem,
):
    bands, rows, cols = obs_ref.shape
    blocks = cols // LANES
    total = bands * rows
    channels = head_ref.shape[1]
    s = lax.axis_index("space")
    p = lax.axis_index("particle")
    me = s * parts + p
    count = strips * parts
    has_low = s > 0
    has_high = s < strips - 1

    fetches = [
        pltpu.make_async_copy(src, dst, in_sem.at[at])
        for at, (src, dst) in enumerate((
            (states_hbm, states_ref), (w1_hbm, w1_ref), (psf_hbm, psf_ref), (b1_hbm, b1_ref),
            (b2_hbm, b2_ref), (w2_hbm, w2_ref), (head_hbm, head_ref), (anc_hbm, anc_ref),
            (carried_hbm, carried_ref), (obs_hbm, obs_ref), (iv_hbm, iv_ref),
            (ids_hbm, ids_h.at[2]), (noise_hbm, noise_ref),
        ))
    ]
    fetches[0].start()

    barrier = pltpu.get_barrier_semaphore()

    def wrapped(at, size):
        return jnp.where(at >= size, at - size, at)

    def ahead(k):
        return wrapped(s + k // parts, strips), wrapped(p + k % parts, parts)

    def behind(k):
        return wrapped(s + (strips - k // parts), strips), wrapped(p + (parts - k % parts), parts)

    def greet(k):
        ts, tp = ahead(k)
        pl.semaphore_signal(
            barrier, inc=1, device_id={"space": ts, "particle": tp}, device_id_type=MESH
        )

    each(1, count, greet)
    for fetch in fetches[1:]:
        fetch.start()

    fetches[0].wait()
    state = states_ref[0].reshape(total, cols)
    high_part = state.astype(jnp.bfloat16)
    hi_g[p] = high_part
    lo_g[p] = (state - high_part.astype(jnp.float32)).astype(jnp.bfloat16)
    pl.semaphore_wait(barrier, count - 1)

    def gather_copy(buf, send, recv, q):
        return pltpu.make_async_remote_copy(
            src_ref=buf.at[p], dst_ref=buf.at[p],
            send_sem=send.at[q], recv_sem=recv.at[p],
            device_id={"particle": q}, device_id_type=MESH,
        )

    def gather_arrival(buf, send, recv, q):
        return pltpu.make_async_remote_copy(
            src_ref=buf.at[q], dst_ref=buf.at[q],
            send_sem=send.at[q], recv_sem=recv.at[q],
            device_id={"particle": q}, device_id_type=MESH,
        )

    def each_other(act):
        for i in range(parts):
            q = jnp.where(p < parts // 2, parts - 1 - i, i)

            @pl.when(p != q)
            def _():
                act(q)

    each_other(lambda q: gather_copy(hi_g, hi_send, hi_recv, q).start())

    def halo(kind, src, dst, side):
        towards = s + 1 if side == 0 else s - 1
        return pltpu.make_async_remote_copy(
            src_ref=src[side], dst_ref=dst.at[side],
            send_sem=halo_send.at[kind, side], recv_sem=halo_recv.at[kind, side],
            device_id={"space": towards}, device_id_type=MESH,
        )

    def start_side(kind, src, dst, side):
        @pl.when(has_high if side == 0 else has_low)
        def _():
            halo(kind, src, dst, side).start()

    def await_side(kind, src, dst, side):
        @pl.when(has_low if side == 0 else has_high)
        def _():
            halo(kind, src, dst, side).wait_recv()

    def start_halo(kind, src, dst):
        for side in range(2):
            start_side(kind, src, dst, side)

    def await_halo(kind, src, dst):
        for side in range(2):
            await_side(kind, src, dst, side)

    def end_halo(kind, src, dst):
        @pl.when(has_high)
        def _():
            halo(kind, src, dst, 0).wait_send()

        @pl.when(has_low)
        def _():
            halo(kind, src, dst, 1).wait_send()

    edge_src = (edge_s.at[0], edge_s.at[1])
    est_src = (est_s.at[0], est_s.at[1])

    def blank(buf, side):
        buf[side] = jnp.zeros(buf.shape[1:], buf.dtype)

    for buf in (edge_h, est_h, obs_h, iv_h, ids_h):
        @pl.when(jnp.logical_not(has_low))
        def _():
            blank(buf, 0)

        @pl.when(jnp.logical_not(has_high))
        def _():
            blank(buf, 1)

    for fetch in fetches[1:]:
        fetch.wait()
    start_halo(4, (ids_h.at[2],) * 2, ids_h)
    start_halo(2, (obs_ref,) * 2, obs_h)
    start_halo(3, (iv_ref,) * 2, iv_h)
    w1t[...] = jnp.zeros(w1t.shape, jnp.float32)
    for band in range(bands):
        for dy in range(3):
            for dx in range(3):
                line = w1_ref[band, dy, dx:dx + 1, :].astype(jnp.float32)
                for half in range(2):
                    at = (dy + half) * 24 + dx * 8 + band
                    w1t[at:at + 1, half * channels:(half + 1) * channels] = line
    w1k[...] = w1t[...].astype(jnp.bfloat16)
    w2s[...] = jnp.zeros(w2s.shape, jnp.bfloat16)
    for dy in range(3):
        for dx in range(3):
            block = w2_ref[dy, dx].T
            for half in range(2):
                at = ((dy + half) * 3 + dx) * channels
                w2s[at:at + channels, half * channels:(half + 1) * channels] = block
    head2[...] = jnp.zeros(head2.shape, jnp.float32)
    for half in range(2):
        head2[half * 8:half * 8 + bands, half * channels:(half + 1) * channels] = head_ref[...].astype(jnp.float32)
        bias[0:1, half * channels:(half + 1) * channels] = b1_ref[...]
        bias[1:2, half * channels:(half + 1) * channels] = b2_ref[...]
    for half in range(2):
        padded[half, 0:8] = jnp.zeros((8, channels), jnp.float32)
        padded[half, 8 + cols:16 + cols] = jnp.zeros((8, channels), jnp.float32)
    bank = psf_ref[...]
    taps, kinds = bank.shape[0] * bank.shape[1], bank.shape[2]
    flat = bank.reshape(taps * kinds, bands)
    eye = (
        lax.broadcasted_iota(jnp.int32, (8, bands), 0)
        == lax.broadcasted_iota(jnp.int32, (8, bands), 1)
    ).astype(jnp.float32)
    columns = lax.dot_general(
        eye, flat, (((1,), (1,)), ((), ())),
        precision=lax.Precision.HIGHEST, preferred_element_type=jnp.float32,
    )
    for tap in range(taps):
        for kind in range(kinds):
            at = tap * kinds + kind
            table[kind, tap] = jnp.broadcast_to(columns[:, at:at + 1], (8, LANES))
    corr[...] = jnp.zeros(corr.shape, jnp.float32)
    obs_t[...] = jnp.zeros(obs_t.shape, jnp.float32)
    iv_t[...] = jnp.zeros(iv_t.shape, jnp.float32)
    lo_rows[...] = jnp.zeros(lo_rows.shape, jnp.float32)
    xc[...] = jnp.zeros(xc.shape, jnp.float32)

    def turned(x):
        return jnp.transpose(x, (1, 0, 2))

    def rows_of(flat_part):
        return turned(flat_part.astype(jnp.float32).reshape(bands, rows, cols))

    def fill_inputs(slot, part):
        value = rows_of(part)
        base = slot * rows
        for dx in range(3):
            xc[base:base + rows, dx * 8:dx * 8 + bands, :] = shifted(value, dx - 1)

    def first_layer(i, masks):
        window = xc[pl.ds(i - 1, 4)].reshape(96, cols).astype(jnp.bfloat16)
        mixed = lax.dot_general(
            window, w1k[...], (((0,), (0,)), ((), ())), preferred_element_type=jnp.float32
        )
        value = silu(mixed + bias[0:1, :])
        for half in range(2):
            part = value[:, half * channels:(half + 1) * channels]
            if masks[half] is not None:
                part = jnp.where(masks[half], part, 0.0)
            padded[half, 8:8 + cols] = part
            at = (i - 7 + half) * cols
            for dx in range(3):
                feats[at:at + cols, dx * channels:(dx + 1) * channels] = (
                    padded[half, 7 + dx:7 + dx + cols].astype(jnp.bfloat16)
                )

    def second_layer(outs):
        window = jnp.concatenate([
            jnp.concatenate([feats[(e - 4 + r) * cols:(e - 3 + r) * cols, :] for r in range(4)], axis=1)
            for e in outs
        ], axis=0)
        mixed = jnp.dot(window, w2s[...], preferred_element_type=jnp.float32)
        hidden = silu(mixed + bias[1:2, :]).astype(jnp.bfloat16)
        both = lax.dot_general(
            head2[...].astype(jnp.bfloat16), hidden, (((1,), (1,)), ((), ())),
            preferred_element_type=jnp.float32,
        )
        for at, e in enumerate(outs):
            corr[e:e + 2] = both[:, at * cols:(at + 1) * cols].reshape(2, 8, cols)

    each_other(lambda q: gather_arrival(hi_g, hi_send, hi_recv, q).wait_recv())
    ancestor = anc_ref[0, 0]
    picked_hi = hi_g[ancestor]
    fill_inputs(1, picked_hi)
    edge_s[0] = xc[14:16, 8:16, :].reshape(16, cols).astype(jnp.bfloat16)
    edge_s[1] = xc[8:10, 8:16, :].reshape(16, cols).astype(jnp.bfloat16)
    start_halo(0, edge_src, edge_h)
    each_other(lambda q: gather_copy(lo_g, lo_send, lo_recv, q).start())
    for i in (9, 11, 13):
        first_layer(i, (None, None))

    second_layer((6, 8))
    deep = 6 * channels

    def half_layer(e, first):
        window = jnp.concatenate(
            [feats[(e - 4 + r) * cols:(e - 3 + r) * cols, :] for r in (first, first + 1)], axis=1
        )
        return jnp.dot(
            window, w2s[first * 3 * channels:first * 3 * channels + deep, :],
            preferred_element_type=jnp.float32,
        )

    begun[0] = half_layer(4, 2)
    begun[1] = half_layer(10, 0)
    await_halo(0, edge_src, edge_h)
    for side, base in ((0, 6), (1, 16)):
        value = edge_h[side].astype(jnp.float32).reshape(2, 8, cols)
        for dx in range(3):
            xc[base:base + 2, dx * 8:dx * 8 + 8, :] = shifted(value, dx - 1)
    first_layer(7, (has_low, None))
    first_layer(15, (None, has_high))
    def rough(e):
        return (xc[e + 4, 8:16, :] - NOISE_ROOT * corr[e]) / ALPHA_ROOT

    mixed = [begun[at] + half_layer(e, first) for at, e, first in ((0, 4, 0), (1, 10, 2))]
    for at, e, side, base in ((0, 4, 1, 4), (1, 10, 0, 8)):
        hidden = silu(mixed[at] + bias[1:2, :]).astype(jnp.bfloat16)
        both = lax.dot_general(
            head2[...].astype(jnp.bfloat16), hidden, (((1,), (1,)), ((), ())),
            preferred_element_type=jnp.float32,
        )
        corr[e:e + 2] = both.reshape(2, 8, cols)
        est_s[side] = jnp.concatenate([rough(base + r) for r in range(4)], axis=0).astype(jnp.bfloat16)
        start_side(1, est_src, est_h, side)

    each_other(lambda q: gather_arrival(lo_g, lo_send, lo_recv, q).wait_recv())
    lo_rows[rows:2 * rows, 0:bands, :] = rows_of(lo_g[ancestor])
    await_halo(4, (ids_h.at[2],) * 2, ids_h)
    ids_copy = pltpu.make_async_copy(ids_h, ids_s, own_sem)
    ids_copy.start()
    await_halo(2, (obs_ref,) * 2, obs_h)
    await_halo(3, (iv_ref,) * 2, iv_h)
    for held, halo_buf, own in ((obs_t, obs_h, obs_ref), (iv_t, iv_h, iv_ref)):
        held[0:2, 0:bands, :] = turned(halo_buf[0])[rows - 2:rows]
        held[2:2 + rows, 0:bands, :] = turned(own[...])
        held[2 + rows:4 + rows, 0:bands, :] = turned(halo_buf[1])[0:2]

    def spread_row(e, value):
        for dx in range(5):
            shifts[e, dx] = shifted(value, dx - 2)

    def estimate_row(e):
        current = xc[e + 4, 8:16, :] + lo_rows[e + 4]
        spread_row(e, (current - NOISE_ROOT * corr[e]) / ALPHA_ROOT)

    def kind_of(q, j):
        low, high = q < 2, q >= 2 + rows
        slot = jnp.where(low, 0, jnp.where(high, 1, 2))
        row = jnp.where(low, rows - 2 + q, jnp.where(high, q - 2 - rows, q - 2))
        return ids_s[slot, j, row]

    def residual_row(q):
        for j in range(blocks):
            kind = kind_of(q, j)
            lanes = slice(j * LANES, (j + 1) * LANES)
            sums = []
            for dy in range(5):
                term = None
                for dx in range(5):
                    product = table[kind, dy * 5 + dx] * shifts[q + dy, dx, :, lanes]
                    term = product if term is None else term + product
                sums.append(term)
            blurred = sums[0] + sums[1] + sums[2] + sums[3] + sums[4]
            misfit = obs_t[q, :, lanes] - blurred
            residual = iv_t[q, :, lanes] * misfit
            if q < 2:
                residual = jnp.where(has_low, residual, 0.0)
            if q >= 2 + rows:
                residual = jnp.where(has_high, residual, 0.0)
            resid[q, :, lanes] = residual
            obs_t[q, :, lanes] = residual * misfit

    for e in range(4, 12):
        estimate_row(e)
    ids_copy.wait()
    for q in range(4, 8):
        residual_row(q)
    for side, base, reach in ((1, 12, range(8, 12)), (0, 0, range(0, 4))):
        await_side(1, est_src, est_h, side)
        for r in range(4):
            spread_row(base + r, est_h[side, r * 8:r * 8 + 8, :].astype(jnp.float32))
        for q in reach:
            residual_row(q)

    def adjoint(y, twist):
        moved = []
        for dx in range(5):
            pieces = []
            for j in range(blocks):
                lanes = slice(j * LANES, (j + 1) * LANES)
                term = None
                for dy in range(5):
                    q = y + 4 - dy
                    product = table[kind_of(q, j), dy * 5 + dx] * resid[q, :, lanes]
                    term = product if term is None else term + product
                pieces.append(term)
            moved.append(shifted(jnp.concatenate(pieces, axis=1), 2 - dx))
        gradient = moved[0] + moved[1] + moved[2] + moved[3] + moved[4]
        corr[y] = shifts[y + 4, 2] + GUIDE * gradient
        return twist + gradient * gradient

    twist = functools.reduce(lambda twist, y: adjoint(y, twist), range(rows), jnp.zeros((8, cols), jnp.float32))
    energy = jnp.sum(obs_t[2:2 + rows], axis=0)
    mixed = -0.5 * energy + (0.5 * GUIDE) * twist
    partial = jnp.sum(mixed, axis=(0, 1), keepdims=True)
    temper = 1.0 / math.sqrt(bands * rows * strips * cols)
    prior = jnp.where(has_low, 0.0, carried_ref[0])
    packs[me] = jnp.broadcast_to(partial * temper, (1, LANES)) + prior

    def pack_copy(k):
        tp, ts = k // strips, wrapped(s + k % strips, strips)
        return ts * parts + tp, pltpu.make_async_remote_copy(
            src_ref=packs.at[me], dst_ref=packs.at[me],
            send_sem=pack_send.at[k], recv_sem=pack_recv.at[me],
            device_id={"space": ts, "particle": tp}, device_id_type=MESH,
        )

    def send_pack(k):
        t, copy = pack_copy(k)

        @pl.when(t != me)
        def _():
            copy.start()

    def end_pack(k):
        t, copy = pack_copy(k)

        @pl.when(t != me)
        def _():
            copy.wait_send()

    def pack_arrival(k):
        ts, tp = behind(k)
        t = ts * parts + tp
        return pltpu.make_async_remote_copy(
            src_ref=packs.at[t], dst_ref=packs.at[t],
            send_sem=pack_send.at[k], recv_sem=pack_recv.at[t],
            device_id={"space": ts, "particle": tp}, device_id_type=MESH,
        )

    each(0, count, send_pack)

    moved = turned(corr[0:rows])
    out_ref[0] = moved[0:bands] + SPREAD * noise_ref[0]

    each_other(lambda q: gather_copy(hi_g, hi_send, hi_recv, q).wait_send())
    each_other(lambda q: gather_copy(lo_g, lo_send, lo_recv, q).wait_send())
    end_halo(0, edge_src, edge_h)
    end_halo(1, est_src, est_h)
    end_halo(2, (obs_ref,) * 2, obs_h)
    end_halo(3, (iv_ref,) * 2, iv_h)
    end_halo(4, (ids_h.at[2],) * 2, ids_h)

    each(0, count, end_pack)
    each(1, count, lambda k: pack_arrival(k).wait_recv())
    raw = packs[0:parts]
    mine = packs[p]
    for strip in range(1, strips):
        raw = raw + packs[strip * parts:(strip + 1) * parts]
        mine = mine + packs[strip * parts + p]
    highest = jnp.max(raw, axis=0)
    summed = jnp.sum(jnp.exp(raw - highest[None]), axis=0)
    logw_ref[...] = jnp.broadcast_to(mine - highest - jnp.log(summed), (8, LANES))


def deliver_kernel(moved_ref, logw_ref, out_hbm, logw_hbm, logw_line, sem):
    states_copy = pltpu.make_async_copy(moved_ref, out_hbm, sem.at[0])
    states_copy.start()
    logw_line[...] = logw_ref[0, 0:1]
    logw_copy = pltpu.make_async_copy(logw_line, logw_hbm, sem.at[1])
    logw_copy.start()
    states_copy.wait()
    logw_copy.wait()


def local(
    strips, parts,
    states, noise, observed, inv_var, psf_bank, psf_ids, ancestors, carried,
    stem_w1, stem_b1, stem_w2, stem_b2, head_w,
):
    bands, rows, cols = observed.shape
    channels = stem_w1.shape[0]
    kinds = psf_bank.shape[0]
    count = strips * parts
    flat = (bands * rows, cols)
    vmem = pl.BlockSpec(memory_space=pltpu.VMEM)
    hbm = pl.BlockSpec(memory_space=pltpu.HBM)
    bf, f32 = jnp.bfloat16, jnp.float32
    dma = pltpu.SemaphoreType.DMA
    next_states, log_weight = pl.pallas_call(
        functools.partial(step_kernel, strips, parts),
        out_shape=(
            pltpu.VMEM(states.shape, f32),
            pltpu.VMEM((8, LANES), f32),
        ),
        in_specs=[hbm] * 13,
        out_specs=(vmem, vmem),
        scratch_shapes=[
            pltpu.SMEM((1, 1), jnp.int32),
            pltpu.SMEM((1,), f32),
            pltpu.VMEM(states.shape, f32),
            pltpu.VMEM(states.shape, f32),
            pltpu.VMEM(observed.shape, f32),
            pltpu.VMEM(observed.shape, f32),
            pltpu.VMEM((5, 5, kinds, bands), f32),
            pltpu.VMEM((bands, 3, 3, channels), bf),
            pltpu.VMEM((1, channels), f32),
            pltpu.VMEM((3, 3, channels, channels), bf),
            pltpu.VMEM((1, channels), f32),
            pltpu.VMEM((bands, channels), bf),
            pltpu.VMEM((96, 2 * channels), f32),
            pltpu.VMEM((96, 2 * channels), bf),
            dma((13,)),
            pltpu.VMEM((16, 2 * channels), f32),
            pltpu.VMEM((2, cols + 16, channels), f32),
            pltpu.VMEM((parts,) + flat, bf),
            pltpu.VMEM((parts,) + flat, bf),
            pltpu.VMEM((2, 16, cols), bf),
            pltpu.VMEM((2, 16, cols), bf),
            pltpu.VMEM((2, 32, cols), bf),
            pltpu.VMEM((2, 32, cols), bf),
            pltpu.VMEM((2, bands, rows, cols), f32),
            pltpu.VMEM((2, bands, rows, cols), f32),
            pltpu.VMEM((3, psf_ids.shape[1], rows), jnp.int32),
            pltpu.SMEM((3, psf_ids.shape[1], rows), jnp.int32),
            pltpu.VMEM((count, 1, LANES), f32),
            pltpu.VMEM((3 * rows, 24, cols), f32),
            pltpu.VMEM((3 * rows, 8, cols), f32),
            pltpu.VMEM((2, cols, 2 * channels), f32),
            pltpu.VMEM((10 * cols, 3 * channels), bf),
            pltpu.VMEM((12 * channels, 2 * channels), bf),
            pltpu.VMEM((16, 8, cols), f32),
            pltpu.VMEM((16, 5, 8, cols), f32),
            pltpu.VMEM((kinds, 25, 8, LANES), f32),
            pltpu.VMEM((rows + 4, 8, cols), f32),
            pltpu.VMEM((rows + 4, 8, cols), f32),
            pltpu.VMEM((rows + 4, 8, cols), f32),
            pltpu.VMEM((2, 2 * channels), f32),
            dma((parts,)), dma((parts,)), dma((parts,)), dma((parts,)),
            dma((5, 2)), dma((5, 2)), dma((count,)), dma((count,)), dma,
        ],
        compiler_params=pltpu.CompilerParams(
            collective_id=0, has_side_effects=True, vmem_limit_bytes=(64 << 20) - (176 << 10)
        ),
    )(
        ancestors, carried, states, noise, observed, inv_var,
        jnp.transpose(psf_bank, (2, 3, 0, 1)), psf_ids.T,
        jnp.transpose(stem_w1, (1, 2, 3, 0)), stem_b1.reshape(1, channels), jnp.transpose(stem_w2, (2, 3, 0, 1)),
        stem_b2.reshape(1, channels), head_w,
    )
    return pl.pallas_call(
        deliver_kernel,
        out_shape=(pltpu.HBM(states.shape, f32), pltpu.HBM((1,), f32)),
        in_specs=[vmem] * 2,
        out_specs=(hbm, hbm),
        scratch_shapes=[pltpu.VMEM((1,), f32), dma((2,))],
        compiler_params=pltpu.CompilerParams(vmem_limit_bytes=1 << 20),
    )(next_states, log_weight)


def solution(mesh):
    return jax.shard_map(
        functools.partial(local, mesh.shape["space"], mesh.shape["particle"]),
        mesh=mesh,
        in_specs=(
            P(("tiles", "particle"), None, "space", None),
            P(("tiles", "particle"), None, "space", None),
            P("tiles", "space", None),
            P("tiles", "space", None),
            P("tiles", None, None, None),
            P(("tiles", "space"), None),
            P(("tiles", "particle"), "space"),
            P(("tiles", "particle")),
            P(),
            P(),
            P(),
            P(),
            P(),
        ),
        out_specs=(P(("tiles", "particle"), None, "space", None), P(("tiles", "particle"))),
        check_vma=False,
    )
```
